256 devices in a mesh: rep: 8 (over y_hi, x), exp: 32 (over y_lo, z, core).
Axes of the slice: x: 4, y: 4 (y_hi: 2, y_lo: 2; y = y_hi * 2 + y_lo), z: 8, core: 2. Of those that a mesh axis runs over, the one named last changes fastest.
Arguments:
- features: bfloat16 [32768, 2048], P(('rep', 'exp')), may hold values from -6 to 6
- out_grad: bfloat16 [32768, 2048], P(('rep', 'exp')), may hold values from -1.5 to 1.5
- expert_ids: int32 [32768, 2], P(('rep', 'exp')), may hold values from 0 to 31, all different within a row; in each aligned block of 128 rows (0 to 127, 128 to 255, ...) at most 16 rows name the same one
- gate_probs: bfloat16 [32768, 2], P(('rep', 'exp')), may hold values from 0.049804688 to 0.59765625
- w_gate: bfloat16 [32, 2048, 768], P('exp'), may hold values from -0.125 to 0.125
- w_up: bfloat16 [32, 2048, 768], P('exp'), may hold values from -0.125 to 0.125
- w_down: bfloat16 [32, 2048, 768], P('exp'), may hold values from -0.21875 to 0.21875
Outputs:
- in_grad: bfloat16 [32768, 2048], P(('rep', 'exp'))
- gate_grad: bfloat16 [32768, 2], P(('rep', 'exp'))
- delta_gate: bfloat16 [32, 2048, 768], P('exp', 'rep')
- delta_up: bfloat16 [32, 2048, 768], P('exp', 'rep')
- delta_down: bfloat16 [32, 2048, 768], P('exp', 'rep')
The draws below stay inside these ranges and needn't reach their ends.
Inputs may be any that keep to these rules, and one draw needn't show every extreme that they name: `expert_ids`: the 2 entries of a token name different experts. Among the 128 tokens of one device (aligned blocks in token order) no expert is named by more than 16 entries, and in every draw some expert is named by exactly 16 entries of some device. Every expert is named somewhere.
All inputs are finite; a program needn't handle non-finite values.
Results may differ from the reference program's by a relative error of at most 0.012.
Values may be sent and summed in bfloat16 or wider, within the bound.
A program may use at most 128 MiB of HBM per device.

```python
import math
import jax
import jax.numpy as jnp
import numpy as np
from jax import lax

D = 2048
FF = 768
TOP = 2
TOK_DEV = 128
EXPERTS = 32
CAP = 16
TOKENS = 32768
N_REP = 8
N_EXP = 32


def block_levels(own_key, extent, cuts, least, top_value):
    def one(dim, parts):
        steps = jax.random.uniform(jax.random.fold_in(jax.random.fold_in(own_key, 6), dim), (parts,), jnp.float32, least / len(cuts), top_value / len(cuts))
        return jnp.repeat(jnp.exp(steps), extent[dim] // parts).reshape((-1,) + (1,) * (len(extent) - dim - 1))

    loudness = one(*cuts[0])
    for cut in cuts[1:]:
        loudness = loudness * one(*cut)
    return loudness


def assign_block(stream_key, own, number, rows, count, top, limit, slope):
    order = jax.random.permutation(stream_key, count)
    packed, ordinary = shares(count, rows * top, limit, slope, True), shares(count, rows * top, limit, slope, False)
    places = jnp.arange(count)

    def named(sizes, turn):
        used = int((sizes > 0).sum())
        fixed = max(1, used // 4)
        shifted = fixed + (places - fixed + turn * (used - fixed)) % max(1, count - fixed)
        return jnp.zeros((count,), jnp.int32).at[order[jnp.where(places < fixed, places, shifted)]].set(jnp.asarray(sizes, jnp.int32))

    sizes = jnp.where(number % 4 == 0, named(packed, number // 4), named(ordinary, number - number // 4 - 1))
    mixed = jax.random.permutation(jax.random.fold_in(own, 3), count)
    donor, sink = mixed[0:count // 2 * 2:2], mixed[1:count // 2 * 2:2]
    room = jnp.minimum(sizes[donor] - 1, limit - sizes[sink]) // 2
    room = jnp.where((donor == order[0]) | (sink == order[0]) | (sizes[sink] == 0), 0, jnp.maximum(room, 0))
    shifted = jax.random.randint(jax.random.fold_in(own, 4), (count // 2,), 0, 1 << 20) % (room + 1)
    sizes = sizes.at[donor].add(-shifted).at[sink].add(shifted)
    members = jnp.searchsorted(jnp.cumsum(sizes), jnp.arange(rows * top), side="right").astype(jnp.int32)
    grid = members.reshape(top, rows).T
    grid = grid[jax.random.permutation(jax.random.fold_in(own, 1), rows)]
    turn = jax.random.randint(jax.random.fold_in(own, 2), (rows, 1), 0, top)
    return jnp.take_along_axis(grid, (jnp.arange(top)[None, :] + turn) % top, axis=1)


def shares(count, total, bound, skew, full):
    loads = [(1 << 20) // math.isqrt(rank ** skew) + 1 for rank in range(1, count + 1)]
    largest = bound if full else min(bound, max(-(-total // count), total * loads[0] // sum(loads)))
    least = 1 if total - largest >= count - 1 else 0
    given, surplus = [largest] + [least] * (count - 1), total - largest - least * (count - 1)
    while surplus > 0:
        candidates = [i for i in range(1, count) if given[i] < largest] or [i for i in range(1, count) if given[i] < bound]
        pool, budget = sum([loads[i] for i in candidates]), surplus
        for i in candidates:
            addition = min(bound - given[i], max(1, budget * loads[i] // pool), surplus)
            given[i] = given[i] + addition
            surplus = surplus - addition
    return np.array(given)


def normal_values(stream_key, dims, spread, bound, pieces=(), kind=jnp.bfloat16):
    result = jax.random.normal(stream_key, dims, jnp.float32) * spread
    if len(pieces) > 0:
        result = block_levels(stream_key, dims, pieces, -0.22, 0.18) * result
    return jnp.clip(result, min=-bound, max=bound).astype(kind)


def setup_inputs(seed: int = 0) -> dict:
    key_of = jax.random.split(jax.random.key(seed), 8)
    features = normal_values(key_of[0], (TOKENS, D), 1.0, 6.0, ((0, 256),))
    out_grad = normal_values(key_of[1], (TOKENS, D), 0.25, 1.5, ((0, 256),))
    expert_ids_keys = jax.random.split(jax.random.fold_in(key_of[2], 1), TOKENS // TOK_DEV)
    expert_ids_turns = jax.random.permutation(jax.random.fold_in(key_of[2], 3), TOKENS // TOK_DEV)
    expert_ids = jax.vmap(lambda own, number: assign_block(jax.random.fold_in(key_of[2], 2), own, number, TOK_DEV, EXPERTS, TOP, CAP, 2))(expert_ids_keys, expert_ids_turns).reshape((TOKENS, TOP))
    gate_probs = jnp.clip(jnp.exp(math.log(0.59765625) - 2.4849066 * jax.random.uniform(key_of[3], (TOKENS, TOP), jnp.float32) ** block_levels(key_of[3], (TOKENS, TOP), ((0, 256),), -0.2, 0.2)), 0.049804688, 0.59765625).astype(jnp.bfloat16)
    w_gate = normal_values(key_of[4], (EXPERTS, D, FF), D ** -0.5, 0.125, ((0, 32),))
    w_up = normal_values(key_of[5], (EXPERTS, D, FF), D ** -0.5, 0.125, ((0, 32),))
    w_down = normal_values(key_of[6], (EXPERTS, D, FF), FF ** -0.5, 0.21875, ((0, 32),))
    return {"features": features, "out_grad": out_grad, "expert_ids": expert_ids, "gate_probs": gate_probs, "w_gate": w_gate, "w_up": w_up, "w_down": w_down}


def dot_rows(matrix_a, matrix_b):
    return lax.dot_general(matrix_a, matrix_b, (((0,), (0,)), ((), ())), preferred_element_type=jnp.float32)


def dot_last(matrix_a, matrix_b):
    return lax.dot_general(matrix_a, matrix_b, (((1,), (1,)), ((), ())), preferred_element_type=jnp.float32)


def expert_terms(inputs, gate_mat, up_mat, down_mat):
    rows_x, rows_dy, rows_g = inputs
    pre_gate = jnp.dot(rows_x, gate_mat, preferred_element_type=jnp.float32)
    pre_up = jnp.dot(rows_x, up_mat, preferred_element_type=jnp.float32)
    gate_sig = jax.nn.sigmoid(pre_gate)
    gate_act = pre_gate * gate_sig
    hidden = (gate_act * pre_up).astype(jnp.bfloat16)
    back_grad = jnp.dot(rows_dy, down_mat, preferred_element_type=jnp.float32)
    gate_row = jnp.sum(back_grad * hidden.astype(jnp.float32), axis=1).astype(jnp.bfloat16)
    scaled = (rows_g * rows_dy.astype(jnp.float32)).astype(jnp.bfloat16)
    d_hidden = rows_g * back_grad
    d_gate = (d_hidden * pre_up * gate_sig * (1.0 + pre_gate * (1.0 - gate_sig))).astype(jnp.bfloat16)
    d_up = (d_hidden * gate_act).astype(jnp.bfloat16)
    row_grad = (dot_last(d_gate, gate_mat) + dot_last(d_up, up_mat)).astype(jnp.bfloat16)
    return row_grad, gate_row, hidden, scaled, d_gate, d_up


def rounded(value):
    return lax.optimization_barrier(value.astype(jnp.bfloat16)).astype(jnp.float32)


def reference(features, out_grad, expert_ids, gate_probs, w_gate, w_up, w_down):
    block = N_EXP * TOK_DEV
    slot_total = N_EXP * CAP
    feats = features.reshape(N_REP, block, D)
    grads = out_grad.reshape(N_REP, block, D)
    gates = gate_probs.reshape(N_REP, block, TOP)
    routes = expert_ids.reshape(N_REP, block * TOP)
    entries = jnp.arange(block * TOP, dtype=jnp.int32)

    def per_expert(carry, expert):
        in_acc, gate_acc = carry
        sum_gate = jnp.zeros((D, FF), jnp.float32)
        sum_up = jnp.zeros((D, FF), jnp.float32)
        sum_down = jnp.zeros((D, FF), jnp.float32)
        for replica in range(N_REP):
            chosen = routes[replica] == expert
            position = jnp.cumsum(chosen.astype(jnp.int32)) - 1
            target = jnp.where(chosen, position, slot_total).astype(jnp.int32)
            picked = jnp.zeros((slot_total + 1,), jnp.int32).at[target].set(entries)[:slot_total]
            valid = jnp.zeros((slot_total + 1,), jnp.float32).at[target].set(1.0)[:slot_total]
            token_idx = (picked // TOP).astype(jnp.int32)
            rank_idx = (picked % TOP).astype(jnp.int32)
            keep = valid.astype(jnp.bfloat16)[:, None]
            rows_x = feats[replica][token_idx] * keep
            rows_dy = grads[replica][token_idx] * keep
            rows_g = (gates[replica][token_idx, rank_idx].astype(jnp.float32) * valid)[:, None]
            row_grad, gate_row, hidden, scaled, d_gate, d_up = expert_terms(
                (rows_x, rows_dy, rows_g), w_gate[expert], w_up[expert], w_down[expert])
            in_acc = in_acc.at[replica, token_idx].add(row_grad.astype(jnp.float32) * valid[:, None])
            gate_acc = gate_acc.at[replica, token_idx, rank_idx].add(gate_row.astype(jnp.float32) * valid)
            sum_gate = sum_gate + rounded(dot_rows(rows_x, d_gate))
            sum_up = sum_up + rounded(dot_rows(rows_x, d_up))
            sum_down = sum_down + rounded(dot_rows(scaled, hidden))
        deltas = ((sum_gate / N_REP).astype(jnp.bfloat16), (sum_up / N_REP).astype(jnp.bfloat16),
                  (sum_down / N_REP).astype(jnp.bfloat16))
        return (in_acc, gate_acc), deltas

    start = (jnp.zeros((N_REP, block, D), jnp.float32), jnp.zeros((N_REP, block, TOP), jnp.float32))
    (in_acc, gate_acc), stacked = lax.scan(per_expert, start, jnp.arange(EXPERTS, dtype=jnp.int32))
    in_grad = in_acc.reshape(TOKENS, D).astype(jnp.bfloat16)
    gate_grad = gate_acc.reshape(TOKENS, TOP).astype(jnp.bfloat16)
    return in_grad, gate_grad, stacked[0], stacked[1], stacked[2]
```

```python
import functools

import jax
import jax.numpy as jnp
from jax import lax
from jax.experimental import pallas as pl
from jax.experimental.pallas import tpu as pltpu
from jax.sharding import PartitionSpec as P

MESH = pl.DeviceIdType.MESH
F32 = jnp.float32
BF16 = jnp.bfloat16
TOK = 128
D = 2048
FF = 768
CAP = 16
NCH = 8
CW = D // NCH
SLOTS = 512
QS = ((0, 0), (0, 1), (1, 0), (1, 1))
BLOCKS = tuple(
    [(dy, dz, dc) for dy, dc in QS for dz in (0, -1, 1, -2, 2)]
    + [(dy, -3, dc) for dy, dc in QS]
    + [(dy, 3, dc) for dy, dc in QS]
    + [(0, 4, dc) for dc in (0, 1)]
    + [(1, 4, dc) for dc in (0, 1)]
)


def kernel(
    feat, og, meta, ids_col, wg, wu, wd,
    ig_out, gg_out, dl_out,
    src, msrc, s1, s2, stg1, stg2, stg3, stg4, gs1, gs2, gs3, gs4, rbuf, gbuf,
    wbuf, acc, acts, rg, ret, a2, ap, am, a0, rp, rm, ysend, yrecv,
    load_sem, w_sem, m_send, m_recv, ring_send, r1, r2, st_send, rx, gsend, grecv,
    a2_send, d_send, c_send, rp_sem, rm_sem, y_send, y_sem, ret_send, ret_sem,
):
    rep = lax.axis_index("rep")
    exp = lax.axis_index("exp")
    x = lax.rem(rep, 4)
    yh = rep // 4
    yl = exp // 16
    z = lax.rem(exp // 2, 8)
    c = lax.rem(exp, 2)

    def exp_of(dy, dz, dc):
        return lax.rem(yl + dy, 2) * 16 + lax.rem(z + dz + 8, 8) * 2 + lax.rem(c + dc, 2)

    def near(dy, dz, dc):
        return {"rep": rep, "exp": exp_of(dy, dz, dc)}

    xp = {"rep": yh * 4 + lax.rem(x + 1, 4), "exp": exp}
    xm = {"rep": yh * 4 + lax.rem(x + 3, 4), "exp": exp}
    yo = {"rep": (1 - yh) * 4 + x, "exp": exp}

    def send(a, b, ss, rs, to):
        pltpu.make_async_remote_copy(
            src_ref=a, dst_ref=b, send_sem=ss, recv_sem=rs, device_id=to, device_id_type=MESH
        ).start()

    def local(a, b, sem):
        pltpu.make_async_copy(a, b, sem).start()

    def wait(ref, sem):
        pltpu.make_async_copy(ref, ref, sem).wait()

    for k in range(NCH):
        cols = pl.ds(k * CW, CW)
        local(feat.at[:, cols], src.at[0, k, :, pl.ds(0, CW)], load_sem.at[k])
        local(og.at[:, cols], src.at[0, k, :, pl.ds(CW, CW)], load_sem.at[k])
    for m, w in enumerate((wg, wu, wd)):
        local(w.at[0], wbuf.at[m], w_sem.at[m])

    barrier = pltpu.get_barrier_semaphore()
    peers = [near(*b) for b in BLOCKS if b != (0, 0, 0)] + [xp, xm, yo]
    for p in peers:
        pl.semaphore_signal(barrier, inc=1, device_id=p, device_id_type=MESH)
    pl.semaphore_wait(barrier, len(peers))

    up, down = near(0, 1, 0), near(0, -1, 0)
    send(meta, msrc.at[0], m_send.at[0], m_recv.at[0], up)
    send(meta, msrc.at[1], m_send.at[1], m_recv.at[1], down)
    for k in range(NCH):
        wait(src.at[0, k], load_sem.at[k])
        send(src.at[0, k], src.at[1, k], ring_send.at[0], r1.at[0, k], up)
        send(src.at[0, k], src.at[2, k], ring_send.at[1], r1.at[1, k], down)

    row_i = lax.broadcasted_iota(jnp.int32, (TOK, TOK), 0)
    col_i = lax.broadcasted_iota(jnp.int32, (TOK, TOK), 1)
    before = jnp.where(row_i < col_i, 1.0, 0.0).astype(BF16)
    slot_i = lax.broadcasted_iota(jnp.int32, (CAP, TOK), 0).astype(F32)

    def pick(meta_v, experts):
        i0, i1, g0, g1 = [jnp.broadcast_to(meta_v[i : i + 1, :], (CAP, TOK)) for i in range(4)]
        rows, gates = [], []
        for e in experts:
            ef = e.astype(F32)
            m0, m1 = i0 == ef, i1 == ef
            hit = jnp.where(m0 | m1, 1.0, 0.0)
            pos = jnp.dot(hit.astype(BF16), before, preferred_element_type=F32)
            one = jnp.where(pos == slot_i, hit, 0.0)
            gate = jnp.sum(one * jnp.where(m0, g0, jnp.where(m1, g1, 0.0)), axis=1, keepdims=True)
            rows.append(one.astype(BF16))
            gates.append(jnp.broadcast_to(gate, (CAP, TOK)).astype(BF16))
        return rows, gates

    own_plane = [exp_of(dy, 0, dc) for dy, dc in QS]

    def plan_first(s, meta_v):
        rows, gates = pick(meta_v, own_plane)
        for q in range(4):
            s1[s, pl.ds(q * CAP, CAP), :] = rows[q]
            gs1[q, pl.ds(s * CAP, CAP), :] = gates[q]

    plan_first(0, meta[...])
    wait(msrc.at[0], m_recv.at[0])
    send(msrc.at[0], msrc.at[2], m_send.at[2], m_recv.at[2], up)
    wait(msrc.at[1], m_recv.at[1])
    send(msrc.at[1], msrc.at[3], m_send.at[3], m_recv.at[3], down)
    plan_first(1, msrc[0])
    plan_first(2, msrc[1])

    def first(k, carry):
        wait(src.at[1, k], r1.at[0, k])
        send(src.at[1, k], src.at[3, k], ring_send.at[2], r2.at[0, k], up)
        wait(src.at[2, k], r1.at[1, k])
        send(src.at[2, k], src.at[4, k], ring_send.at[3], r2.at[1, k], down)
        for s in range(3):
            got = jnp.dot(s1[s], src[s, k], preferred_element_type=F32).astype(BF16)
            for q in range(4):
                stg1[q, k, pl.ds(s * CAP, CAP), :] = got[q * CAP : (q + 1) * CAP]
        local(stg1.at[0, k], rbuf.at[k, pl.ds(0, 48)], rx.at[k])
        for q in range(1, 4):
            send(stg1.at[q, k], rbuf.at[k, pl.ds(q * 80, 48)], st_send.at[0], rx.at[k], near(QS[q][0], 0, QS[q][1]))
        return carry

    lax.fori_loop(0, NCH, first, 0)

    for d in range(2):
        step = 1 if d == 0 else -1
        wait(msrc.at[2 + d], m_recv.at[2 + d])
        third = [exp_of(dy, step, dc) for dy, dc in QS]
        fourth = [exp_of(d, 2 * step, dc) for dc in (0, 1)]
        rows, gates = pick(msrc[2 + d], own_plane + third + fourth)
        for i in range(10):
            s2[d, pl.ds(i * CAP, CAP), :] = rows[i]
        for q in range(4):
            gs2[q, pl.ds(d * CAP, CAP), :] = gates[q]
            gs3[d, q] = gates[4 + q]
        for i in range(2):
            gs4[d, i] = gates[8 + i]

    def second(k, carry):
        for d in range(2):
            step = 1 if d == 0 else -1
            wait(src.at[3 + d, k], r2.at[d, k])
            got = jnp.dot(s2[d], src[3 + d, k], preferred_element_type=F32).astype(BF16)
            for q in range(4):
                stg3[d, q, k] = got[(4 + q) * CAP : (5 + q) * CAP]
                stg2[q, k, pl.ds(d * CAP, CAP), :] = got[q * CAP : (q + 1) * CAP]
            for i in range(2):
                stg4[d, i, k] = got[(8 + i) * CAP : (9 + i) * CAP]
            for i in range(2):
                send(stg4.at[d, i, k], rbuf.at[k, pl.ds(448 + (d * 2 + i) * CAP, CAP)], st_send.at[3], rx.at[k], near(d, 2 * step, i))
            for q in range(4):
                send(stg3.at[d, q, k], rbuf.at[k, pl.ds(320 + (d * 4 + q) * CAP, CAP)], st_send.at[2], rx.at[k], near(QS[q][0], step, QS[q][1]))
        local(stg2.at[0, k], rbuf.at[k, pl.ds(48, 32)], rx.at[k])
        for q in range(1, 4):
            send(stg2.at[q, k], rbuf.at[k, pl.ds(q * 80 + 48, 32)], st_send.at[1], rx.at[k], near(QS[q][0], 0, QS[q][1]))
        return carry

    lax.fori_loop(0, NCH, second, 0)

    local(gs1.at[0], gbuf.at[pl.ds(0, 48)], grecv)
    local(gs2.at[0], gbuf.at[pl.ds(48, 32)], grecv)
    for q in range(1, 4):
        to = near(QS[q][0], 0, QS[q][1])
        send(gs1.at[q], gbuf.at[pl.ds(q * 80, 48)], gsend.at[0], grecv, to)
        send(gs2.at[q], gbuf.at[pl.ds(q * 80 + 48, 32)], gsend.at[1], grecv, to)
    for d in range(2):
        step = 1 if d == 0 else -1
        for q in range(4):
            send(gs3.at[d, q], gbuf.at[pl.ds(320 + (d * 4 + q) * CAP, CAP)], gsend.at[2], grecv, near(QS[q][0], step, QS[q][1]))
        for i in range(2):
            send(gs4.at[d, i], gbuf.at[pl.ds(448 + (d * 2 + i) * CAP, CAP)], gsend.at[3], grecv, near(d, 2 * step, i))

    for i in range(2):
        wait(src.at[0], ring_send.at[i])
        wait(src.at[1], ring_send.at[2 + i])
    for m in range(3):
        wait(wbuf.at[m], w_sem.at[m])
    wait(gbuf, grecv)

    def forward(k, carry):
        wait(rbuf.at[k], rx.at[k])
        krow = pl.ds(pl.multiple_of(k * CW, CW), CW)
        for m in range(3):
            a = rbuf[k, :, pl.ds(0 if m < 2 else CW, CW)]

            def tile(n, cc, m=m, a=a):
                ncol = pl.ds(pl.multiple_of(n * 256, 256), 256)
                part = jnp.dot(a, wbuf[m, krow, ncol], preferred_element_type=F32)

                @pl.when(k == 0)
                def _():
                    acc[m, :, ncol] = part

                @pl.when(k > 0)
                def _():
                    acc[m, :, ncol] = acc[m, :, ncol] + part

                return cc

            lax.fori_loop(0, FF // 256, tile, 0)
        gcol = gbuf[...].astype(F32)
        for h in range(2):
            src[h, k] = rbuf[k, :, pl.ds(h * TOK, TOK)].T
            dy = rbuf[k, :, pl.ds(CW + h * TOK, TOK)].astype(F32)
            src[2 + h, k] = (gcol * dy).astype(BF16).T
        return carry

    lax.fori_loop(0, NCH, forward, 0)

    def pointwise(i, carry):
        rows = pl.ds(pl.multiple_of(i * 32, 32), 32)
        g = gbuf[rows, pl.ds(0, 1)].astype(F32)
        pg, pu, bg = acc[0, rows, :], acc[1, rows, :], acc[2, rows, :]
        sig = jax.nn.sigmoid(pg)
        act = pg * sig
        hid = (act * pu).astype(BF16)
        gate = jnp.sum(bg * hid.astype(F32), axis=1, keepdims=True)
        dh = g * bg
        acts[0, rows, :] = (dh * pu * sig * (1.0 + pg * (1.0 - sig))).astype(BF16)
        acts[1, rows, :] = (dh * act).astype(BF16)
        acts[2, rows, :] = hid
        rg[rows, pl.ds(D, TOK)] = jnp.broadcast_to(gate, (32, TOK)).astype(BF16)
        return carry

    lax.fori_loop(0, SLOTS // 32, pointwise, 0)

    def product(owner, j):
        half, m = j // 3, lax.rem(j, 3)
        b = lax.rem(yh + 1 + half, 2) * 4 + lax.rem(x + owner, 4)
        w = (m // 2) * 2
        left = jnp.concatenate([src[w, b], src[w + 1, b]], axis=0)
        return jnp.dot(left, acts[m], preferred_element_type=F32).astype(BF16)

    def far(j, carry):
        v = product(2, j)
        a2[0, j] = v[:TOK]
        a2[1, j] = v[TOK:]
        send(a2.at[0, j], rp.at[0, j], a2_send.at[0], rp_sem.at[0, j], xm)
        send(a2.at[1, j], rm.at[0, j], a2_send.at[1], rm_sem.at[0, j], xp)
        return carry

    lax.fori_loop(0, 6, far, 0)

    def beside(j, carry):
        v = product(1, j)
        ap[0, j] = v[:TOK]
        ap[1, j] = v[TOK:]
        v = product(3, j)
        am[0, j] = v[:TOK]
        am[1, j] = v[TOK:]
        return carry

    lax.fori_loop(0, 6, beside, 0)

    def direct(j, carry):
        send(ap.at[0, j], rm.at[1, j], d_send.at[0], rm_sem.at[1, j], xp)
        send(am.at[1, j], rp.at[1, j], d_send.at[1], rp_sem.at[1, j], xm)
        return carry

    def combine(j, carry):
        wait(rm.at[0, j], rm_sem.at[0, j])
        ap[1, j] = (ap[1, j].astype(F32) + rm[0, j].astype(F32)).astype(BF16)
        send(ap.at[1, j], rm.at[2, j], c_send.at[0], rm_sem.at[2, j], xp)
        wait(rp.at[0, j], rp_sem.at[0, j])
        am[0, j] = (am[0, j].astype(F32) + rp[0, j].astype(F32)).astype(BF16)
        send(am.at[0, j], rp.at[2, j], c_send.at[1], rp_sem.at[2, j], xm)
        return carry

    lax.fori_loop(0, 3, direct, 0)

    def back(n, carry):
        nrow = pl.ds(pl.multiple_of(n * 256, 256), 256)
        dims = (((1,), (1,)), ((), ()))
        v = lax.dot_general(acts[0], wbuf[0, nrow, :], dims, preferred_element_type=F32)
        v = v + lax.dot_general(acts[1], wbuf[1, nrow, :], dims, preferred_element_type=F32)
        rg[:, nrow] = v.astype(BF16)
        return carry

    lax.fori_loop(0, D // 256, back, 0)
    for i, b in enumerate(BLOCKS):
        rows = pl.ds(i * CAP, CAP)
        if b == (0, 0, 0):
            local(rg.at[rows], ret.at[rows], ret_sem)
        else:
            send(rg.at[rows], ret.at[rows], ret_send, ret_sem, near(*b))

    lax.fori_loop(0, 3, combine, 0)
    lax.fori_loop(3, 6, direct, 0)

    def mine(j, carry):
        v = product(0, j)
        a0[0, j] = v[:TOK]
        a0[1, j] = v[TOK:]
        return carry

    lax.fori_loop(0, 6, mine, 0)
    lax.fori_loop(3, 6, combine, 0)

    def total(j, h):
        s = a0[h, j].astype(F32) + rp[2 - h, j].astype(F32)
        return s + rm[1 + h, j].astype(F32)

    def arrived(j):
        for i in (1, 2):
            wait(rp.at[i, j], rp_sem.at[i, j])
            wait(rm.at[i, j], rm_sem.at[i, j])

    def across(j, carry):
        arrived(j)
        for h in range(2):
            ysend[j, h] = total(j, h).astype(BF16)
        send(ysend.at[j], yrecv.at[j], y_send, y_sem.at[j], yo)
        return carry

    lax.fori_loop(0, 3, across, 0)

    wait(ret, ret_sem)
    lane = lax.broadcasted_iota(jnp.int32, (1, SLOTS), 1)
    blk = lane // CAP
    expert = jnp.zeros((1, SLOTS), F32)
    for i, (dy, dz, dc) in enumerate(BLOCKS):
        expert = jnp.where(blk == i, exp_of(dy, -dz, dc).astype(F32), expert)
    slot = (lane - blk * CAP).astype(F32)
    h0 = jnp.where(ids_col[:, 0:1] == expert, 1.0, 0.0)
    h1 = jnp.where(ids_col[:, 1:2] == expert, 1.0, 0.0)
    after = jnp.where(row_i > col_i, 1.0, 0.0).astype(BF16)
    pos = jnp.dot(after, (h0 + h1).astype(BF16), preferred_element_type=F32)
    h0 = jnp.where(pos == slot, h0, 0.0).astype(BF16)
    h1 = jnp.where(pos == slot, h1, 0.0).astype(BF16)
    both = h0 + h1

    def gather(n, carry):
        ncol = pl.ds(pl.multiple_of(n * 256, 256), 256)
        ig_out[:, ncol] = jnp.dot(both, ret[:, ncol], preferred_element_type=F32).astype(BF16)
        return carry

    lax.fori_loop(0, D // 256, gather, 0)
    g = ret[:, pl.ds(D, TOK)]
    g0 = jnp.dot(h0, g, preferred_element_type=F32)
    g1 = jnp.dot(h1, g, preferred_element_type=F32)
    gl = lax.broadcasted_iota(jnp.int32, (TOK, TOK), 1)
    gg_out[...] = jnp.where(gl == 0, g0, g1).astype(BF16)

    def finish(j, carry):
        arrived(j)
        wait(yrecv.at[j - 3], y_sem.at[j - 3])
        for h in range(2):
            s = total(j, h) + yrecv[j - 3, h].astype(F32)
            dl_out[j - 3, pl.ds(h * TOK, TOK), :] = (s * 0.125).astype(BF16)
        return carry

    lax.fori_loop(3, 6, finish, 0)

    for i in range(4):
        wait(msrc.at[0], m_send.at[i])
    wait(stg1.at[pl.ds(1, 3)], st_send.at[0])
    wait(stg2.at[pl.ds(1, 3)], st_send.at[1])
    wait(stg3, st_send.at[2])
    wait(stg4, st_send.at[3])
    wait(gs1.at[pl.ds(1, 3)], gsend.at[0])
    wait(gs2.at[pl.ds(1, 3)], gsend.at[1])
    wait(gs3, gsend.at[2])
    wait(gs4, gsend.at[3])
    for i in range(2):
        wait(a2.at[i], a2_send.at[i])
        wait(ap.at[i], d_send.at[i])
        wait(ap.at[i], c_send.at[i])
    wait(ysend, y_send)
    wait(rg.at[pl.ds(CAP, SLOTS - CAP)], ret_send)


def on_device(features, out_grad, expert_ids, gate_probs, w_gate, w_up, w_down):
    ids = expert_ids.astype(F32)
    meta = jnp.concatenate([ids.T, gate_probs.astype(F32).T, jnp.zeros((4, TOK), F32)], axis=0)
    vm, anyspace = pl.BlockSpec(memory_space=pltpu.VMEM), pl.BlockSpec(memory_space=pl.ANY)
    dma = pltpu.SemaphoreType.DMA
    ig, gg, dl = pl.pallas_call(
        kernel,
        name="moe",
        out_shape=(
            jax.ShapeDtypeStruct((TOK, D), BF16),
            jax.ShapeDtypeStruct((TOK, TOK), BF16),
            jax.ShapeDtypeStruct((3, 256, FF), BF16),
        ),
        in_specs=[anyspace, anyspace, vm, vm, anyspace, anyspace, anyspace],
        out_specs=(vm, vm, vm),
        scratch_shapes=[
            pltpu.VMEM((5, NCH, TOK, 2 * CW), BF16),
            pltpu.VMEM((4, 8, TOK), F32),
            pltpu.VMEM((3, 64, TOK), BF16),
            pltpu.VMEM((2, 160, TOK), BF16),
            pltpu.VMEM((4, NCH, 48, 2 * CW), BF16),
            pltpu.VMEM((4, NCH, 32, 2 * CW), BF16),
            pltpu.VMEM((2, 4, NCH, CAP, 2 * CW), BF16),
            pltpu.VMEM((2, 2, NCH, CAP, 2 * CW), BF16),
            pltpu.VMEM((4, 48, TOK), BF16),
            pltpu.VMEM((4, 32, TOK), BF16),
            pltpu.VMEM((2, 4, CAP, TOK), BF16),
            pltpu.VMEM((2, 2, CAP, TOK), BF16),
            pltpu.VMEM((NCH, SLOTS, 2 * CW), BF16),
            pltpu.VMEM((SLOTS, TOK), BF16),
            pltpu.VMEM((3, D, FF), BF16),
            pltpu.VMEM((3, SLOTS, FF), F32),
            pltpu.VMEM((3, SLOTS, FF), BF16),
            pltpu.VMEM((SLOTS, D + TOK), BF16),
            pltpu.VMEM((SLOTS, D + TOK), BF16),
            pltpu.VMEM((2, 6, TOK, FF), BF16),
            pltpu.VMEM((2, 6, TOK, FF), BF16),
            pltpu.VMEM((2, 6, TOK, FF), BF16),
            pltpu.VMEM((2, 6, TOK, FF), BF16),
            pltpu.VMEM((3, 6, TOK, FF), BF16),
            pltpu.VMEM((3, 6, TOK, FF), BF16),
            pltpu.VMEM((3, 2, TOK, FF), BF16),
            pltpu.VMEM((3, 2, TOK, FF), BF16),
            dma((NCH,)),
            dma((3,)),
            dma((4,)),
            dma((4,)),
            dma((4,)),
            dma((2, NCH)),
            dma((2, NCH)),
            dma((4,)),
            dma((NCH,)),
            dma((4,)),
            dma,
            dma((2,)),
            dma((2,)),
            dma((2,)),
            dma((3, 6)),
            dma((3, 6)),
            dma,
            dma((3,)),
            dma,
            dma,
        ],
        compiler_params=pltpu.CompilerParams(
            collective_id=0, has_side_effects=True, vmem_limit_bytes=67_000_000
        ),
    )(features, out_grad, meta, ids, w_gate, w_up, w_down)
    return (ig, gg[:, :2], dl[0:1], dl[1:2], dl[2:3])


def solution(mesh):
    rows = P(("rep", "exp"), None)
    weights = P("exp", None, None)
    deltas = P("exp", "rep", None)
    return jax.shard_map(
        on_device,
        mesh=mesh,
        in_specs=(rows, rows, rows, rows, weights, weights, weights),
        out_specs=(rows, rows, deltas, deltas, deltas),
        check_vma=False,
    )
```

```python
import functools

import jax
import jax.numpy as jnp
from jax import lax
from jax.experimental import pallas as pl
from jax.experimental.pallas import tpu as pltpu
from jax.sharding import PartitionSpec as P

MESH = pl.DeviceIdType.MESH
F32 = jnp.float32
BF16 = jnp.bfloat16
TOK = 128
D = 2048
FF = 768
CAP = 16
NCH = 8
CW = D // NCH
SLOTS = 512
NEAR = 320
BW = 256
NA = 7
NB = 2
NU = 2 * NA + NB
QS = ((0, 0), (0, 1), (1, 0), (1, 1))
BLOCKS = tuple(
    [(dy, dz, dc) for dy, dc in QS for dz in (0, -1, 1, -2, 2)]
    + [(dy, -3, dc) for dy, dc in QS]
    + [(dy, 3, dc) for dy, dc in QS]
    + [(0, 4, dc) for dc in (0, 1)]
    + [(1, 4, dc) for dc in (0, 1)]
)


def kernel(
    feat, og, ids_row, gates_row, wg, wu, wd,
    ig_out, gg_out, dl_out,
    src, mine_meta, msrc, s1, s2, stg1, stg2, stg3, stg4, gs1, gs2, gs3, gs4, rbuf, gbuf,
    wbuf, acc, acts, rg, ret, a2, ap, am, a0, rp, rm, yb_send, yb_recv, ysend, yrecv,
    load_sem, w_sem, m_send, m_recv, ring_send, r1, r2, st_send, rx, rx2, gsend, grecv,
    a2_send, d_send, c_send, rp_sem, rm_sem, yb_ssem, yb_sem, y_send, y_sem, ret_send, ret_sem, hop_sem,
):
    rep = lax.axis_index("rep")
    exp = lax.axis_index("exp")
    x = lax.rem(rep, 4)
    yh = rep // 4
    yl = exp // 16
    z = lax.rem(exp // 2, 8)
    c = lax.rem(exp, 2)

    def exp_of(dy, dz, dc):
        return lax.rem(yl + dy, 2) * 16 + lax.rem(z + dz + 8, 8) * 2 + lax.rem(c + dc, 2)

    def near(dy, dz, dc):
        return {"rep": rep, "exp": exp_of(dy, dz, dc)}

    xp = {"rep": yh * 4 + lax.rem(x + 1, 4), "exp": exp}
    xm = {"rep": yh * 4 + lax.rem(x + 3, 4), "exp": exp}
    yo = {"rep": (1 - yh) * 4 + x, "exp": exp}

    def send(a, b, ss, rs, to):
        pltpu.make_async_remote_copy(
            src_ref=a, dst_ref=b, send_sem=ss, recv_sem=rs, device_id=to, device_id_type=MESH
        ).start()

    def local(a, b, sem):
        pltpu.make_async_copy(a, b, sem).start()

    def wait(ref, sem):
        pltpu.make_async_copy(ref, ref, sem).wait()

    for k in range(NCH):
        cols = pl.ds(k * CW, CW)
        local(feat.at[:, cols], src.at[0, k, :, pl.ds(0, CW)], load_sem.at[k])
        local(og.at[:, cols], src.at[0, k, :, pl.ds(CW, CW)], load_sem.at[k])
    for m, w in enumerate((wg, wu, wd)):
        local(w.at[0], wbuf.at[m], w_sem.at[m])

    mine_meta[...] = jnp.zeros_like(mine_meta)
    mine_meta[0:2, :] = ids_row[...].astype(F32)
    mine_meta[2:4, :] = gates_row[...].astype(F32)

    up, down = near(0, 1, 0), near(0, -1, 0)
    barrier = pltpu.get_barrier_semaphore()
    peers = [up, down] + [near(dy, 0, dc) for dy, dc in QS[1:]] + [xp, xm, yo]
    for p in peers:
        pl.semaphore_signal(barrier, inc=1, device_id=p, device_id_type=MESH)
    pl.semaphore_wait(barrier, len(peers))

    send(mine_meta, msrc.at[0], m_send.at[0], m_recv.at[0], up)
    send(mine_meta, msrc.at[1], m_send.at[1], m_recv.at[1], down)
    for k in range(NCH):
        wait(src.at[0, k], load_sem.at[k])
        send(src.at[0, k], src.at[1, k], ring_send.at[0], r1.at[0, k], up)
        send(src.at[0, k], src.at[2, k], ring_send.at[1], r1.at[1, k], down)

    def greet(i):
        for p in (up, down):
            pl.semaphore_signal(hop_sem.at[i], inc=1, device_id=p, device_id_type=MESH)

    def greeted(i):
        pl.semaphore_wait(hop_sem.at[i], 2)

    greet(0)
    row_i = lax.broadcasted_iota(jnp.int32, (TOK, TOK), 0)
    col_i = lax.broadcasted_iota(jnp.int32, (TOK, TOK), 1)
    before = jnp.where(row_i < col_i, 1.0, 0.0).astype(BF16)
    slot_i = lax.broadcasted_iota(jnp.int32, (CAP, TOK), 0).astype(F32)

    def pick(meta_v, experts):
        i0, i1, g0, g1 = [jnp.broadcast_to(meta_v[i : i + 1, :], (CAP, TOK)) for i in range(4)]
        rows, gates = [], []
        for e in experts:
            ef = e.astype(F32)
            m0, m1 = i0 == ef, i1 == ef
            hit = jnp.where(m0 | m1, 1.0, 0.0)
            pos = jnp.dot(hit.astype(BF16), before, preferred_element_type=F32)
            one = jnp.where(pos == slot_i, hit, 0.0)
            gate = jnp.sum(one * jnp.where(m0, g0, jnp.where(m1, g1, 0.0)), axis=1, keepdims=True)
            rows.append(one.astype(BF16))
            gates.append(jnp.broadcast_to(gate, (CAP, TOK)).astype(BF16))
        return rows, gates

    own_plane = [exp_of(dy, 0, dc) for dy, dc in QS]

    def plan_first(s, meta_v):
        rows, gates = pick(meta_v, own_plane)
        for q in range(4):
            s1[s, pl.ds(q * CAP, CAP), :] = rows[q]
            gs1[q, pl.ds(s * CAP, CAP), :] = gates[q]

    plan_first(0, mine_meta[...])
    for i in range(3):
        greeted(i)
        greet(i + 1)
    wait(msrc.at[0], m_recv.at[0])
    send(msrc.at[0], msrc.at[2], m_send.at[2], m_recv.at[2], up)
    wait(msrc.at[1], m_recv.at[1])
    send(msrc.at[1], msrc.at[3], m_send.at[3], m_recv.at[3], down)
    plan_first(1, msrc[0])
    plan_first(2, msrc[1])
    greeted(3)
    local(gs1.at[0], gbuf.at[pl.ds(0, 48)], grecv.at[0])
    for q in range(1, 4):
        send(gs1.at[q], gbuf.at[pl.ds(q * 80, 48)], gsend.at[0], grecv.at[0], near(QS[q][0], 0, QS[q][1]))

    def first(k, carry):
        wait(src.at[1, k], r1.at[0, k])
        send(src.at[1, k], src.at[3, k], ring_send.at[2], r2.at[0, k], up)
        wait(src.at[2, k], r1.at[1, k])
        send(src.at[2, k], src.at[4, k], ring_send.at[3], r2.at[1, k], down)
        for s in range(3):
            got = jnp.dot(s1[s], src[s, k], preferred_element_type=F32).astype(BF16)
            for q in range(4):
                stg1[q, k, pl.ds(s * CAP, CAP), :] = got[q * CAP : (q + 1) * CAP]
        local(stg1.at[0, k], rbuf.at[k, pl.ds(0, 48)], rx.at[k])
        for q in range(1, 4):
            send(stg1.at[q, k], rbuf.at[k, pl.ds(q * 80, 48)], st_send.at[0], rx.at[k], near(QS[q][0], 0, QS[q][1]))
        return carry

    lax.fori_loop(0, NCH, first, 0)

    for d in range(2):
        step = 1 if d == 0 else -1
        wait(msrc.at[2 + d], m_recv.at[2 + d])
        third = [exp_of(dy, step, dc) for dy, dc in QS]
        fourth = [exp_of(d, 2 * step, dc) for dc in (0, 1)]
        rows, gates = pick(msrc[2 + d], own_plane + third + fourth)
        for i in range(10):
            s2[d, pl.ds(i * CAP, CAP), :] = rows[i]
        for q in range(4):
            gs2[q, pl.ds(d * CAP, CAP), :] = gates[q]
            gs3[d, q] = gates[4 + q]
        for i in range(2):
            gs4[d, i] = gates[8 + i]
    local(gs2.at[0], gbuf.at[pl.ds(48, 32)], grecv.at[0])
    for q in range(1, 4):
        send(gs2.at[q], gbuf.at[pl.ds(q * 80 + 48, 32)], gsend.at[1], grecv.at[0], near(QS[q][0], 0, QS[q][1]))
    for d in range(2):
        step = 1 if d == 0 else -1
        for q in range(4):
            send(gs3.at[d, q], gbuf.at[pl.ds(320 + (d * 4 + q) * CAP, CAP)], gsend.at[2], grecv.at[1], near(QS[q][0], step, QS[q][1]))
        for i in range(2):
            send(gs4.at[d, i], gbuf.at[pl.ds(448 + (d * 2 + i) * CAP, CAP)], gsend.at[3], grecv.at[1], near(d, 2 * step, i))

    def second(k, carry):
        for d in range(2):
            step = 1 if d == 0 else -1
            wait(src.at[3 + d, k], r2.at[d, k])
            got = jnp.dot(s2[d], src[3 + d, k], preferred_element_type=F32).astype(BF16)
            for q in range(4):
                stg3[d, q, k] = got[(4 + q) * CAP : (5 + q) * CAP]
                stg2[q, k, pl.ds(d * CAP, CAP), :] = got[q * CAP : (q + 1) * CAP]
            for i in range(2):
                stg4[d, i, k] = got[(8 + i) * CAP : (9 + i) * CAP]
            for i in range(2):
                send(stg4.at[d, i, k], rbuf.at[k, pl.ds(448 + (d * 2 + i) * CAP, CAP)], st_send.at[3], rx2.at[k], near(d, 2 * step, i))
            for q in range(4):
                send(stg3.at[d, q, k], rbuf.at[k, pl.ds(320 + (d * 4 + q) * CAP, CAP)], st_send.at[2], rx2.at[k], near(QS[q][0], step, QS[q][1]))
        local(stg2.at[0, k], rbuf.at[k, pl.ds(48, 32)], rx.at[k])
        for q in range(1, 4):
            send(stg2.at[q, k], rbuf.at[k, pl.ds(q * 80 + 48, 32)], st_send.at[1], rx.at[k], near(QS[q][0], 0, QS[q][1]))
        return carry

    lax.fori_loop(0, NCH, second, 0)

    for i in range(2):
        wait(src.at[0], ring_send.at[i])
        wait(src.at[1], ring_send.at[2 + i])
    for m in range(3):
        wait(wbuf.at[m], w_sem.at[m])
    wait(gbuf.at[pl.ds(0, NEAR)], grecv.at[0])
    for k in range(NCH):
        wait(rbuf.at[k, pl.ds(0, NEAR)], rx.at[k])

    def near_rows(n, carry):
        ncol = pl.ds(pl.multiple_of(n * 256, 256), 256)
        for m in range(3):
            c0 = 0 if m < 2 else CW
            v = jnp.zeros((NEAR, 256), F32)
            for k in range(NCH):
                v = v + jnp.dot(
                    rbuf[k, pl.ds(0, NEAR), pl.ds(c0, CW)],
                    wbuf[m, pl.ds(k * CW, CW), ncol],
                    preferred_element_type=F32,
                )
            acc[m, pl.ds(0, NEAR), ncol] = v
        return carry

    lax.fori_loop(0, FF // 256, near_rows, 0)

    def turn(k, r0):
        rows = pl.ds(r0, 256)
        gcol = gbuf[rows, :].astype(F32)
        for h in range(2):
            src[h, k, :, rows] = rbuf[k, rows, pl.ds(h * TOK, TOK)].T
            dy = rbuf[k, rows, pl.ds(CW + h * TOK, TOK)].astype(F32)
            src[2 + h, k, :, rows] = (gcol * dy).astype(BF16).T

    def turn_first(k, carry):
        turn(k, 0)
        return carry

    lax.fori_loop(0, NCH, turn_first, 0)

    def pointwise(i, carry):
        rows = pl.ds(pl.multiple_of(i * 32, 32), 32)
        g = gbuf[rows, pl.ds(0, 1)].astype(F32)
        pg, pu, bg = acc[0, rows, :], acc[1, rows, :], acc[2, rows, :]
        sig = jax.nn.sigmoid(pg)
        act = pg * sig
        hid = (act * pu).astype(BF16)
        gate = jnp.sum(bg * hid.astype(F32), axis=1, keepdims=True)
        dh = g * bg
        d_gate = (dh * pu * sig * (1.0 + pg * (1.0 - sig))).astype(BF16)
        d_up = (dh * act).astype(BF16)
        for n in range(FF // BW):
            cols = slice(n * BW, (n + 1) * BW)
            acts[n, rows, :] = d_gate[:, cols]
            acts[3 + n, rows, :] = d_up[:, cols]
            acts[6 + n, rows, :] = hid[:, cols]
        rg[rows, pl.ds(D, TOK)] = jnp.broadcast_to(gate, (32, TOK)).astype(BF16)
        return carry

    lax.fori_loop(0, NEAR // 32, pointwise, 0)

    wait(gbuf.at[pl.ds(NEAR, SLOTS - NEAR)], grecv.at[1])
    rest = pl.ds(NEAR, SLOTS - NEAR)

    def far_rows(k, carry):
        wait(rbuf.at[k, rest], rx2.at[k])
        krow = pl.ds(pl.multiple_of(k * CW, CW), CW)
        for m in range(3):
            a = rbuf[k, rest, pl.ds(0 if m < 2 else CW, CW)]
            part = jnp.dot(a, wbuf[m, krow, :], preferred_element_type=F32)

            @pl.when(k == 0)
            def _():
                acc[m, rest, :] = part

            @pl.when(k > 0)
            def _():
                acc[m, rest, :] = acc[m, rest, :] + part

        turn(k, 256)
        return carry

    lax.fori_loop(0, NCH, far_rows, 0)
    lax.fori_loop(NEAR // 32, SLOTS // 32, pointwise, 0)

    def product(owner, half, n):
        b = lax.rem(yh + 1 + half, 2) * 4 + lax.rem(x + owner, 4)
        w = (n // 6) * 2
        left = jnp.concatenate([src[w, b], src[w + 1, b]], axis=0)
        return jnp.dot(left, acts[n], preferred_element_type=F32)

    def put(ref, u, v):
        v = v.astype(BF16)
        ref[0, u] = v[:TOK]
        ref[1, u] = v[TOK:]

    def send_far(u):
        send(a2.at[0, u], rp.at[0, u], a2_send.at[0], rp_sem.at[0, u], xm)
        send(a2.at[1, u], rm.at[0, u], a2_send.at[1], rm_sem.at[0, u], xp)

    def far(u, carry):
        put(a2, u, product(2, u // NA, lax.rem(u, NA)))
        send_far(u)
        return carry

    lax.fori_loop(0, 2 * NA, far, 0)

    def to_y(i, carry):
        o, n = i // NB, lax.rem(i, NB)
        yb_send[o, n] = product(o, 0, NA + n).astype(BF16)
        send(yb_send.at[o, n], yb_recv.at[o, n], yb_ssem, yb_sem, yo)
        return carry

    lax.fori_loop(0, 4 * NB, to_y, 0)

    def beside(u, carry):
        put(ap, u, product(1, u // NA, lax.rem(u, NA)))
        put(am, u, product(3, u // NA, lax.rem(u, NA)))
        return carry

    lax.fori_loop(0, 2 * NA, beside, 0)

    def direct(u, carry):
        send(ap.at[0, u], rm.at[1, u], d_send.at[0], rm_sem.at[1, u], xp)
        send(am.at[1, u], rp.at[1, u], d_send.at[1], rp_sem.at[1, u], xm)
        return carry

    def combine(u, carry):
        wait(rm.at[0, u], rm_sem.at[0, u])
        ap[1, u] = (ap[1, u].astype(F32) + rm[0, u].astype(F32)).astype(BF16)
        send(ap.at[1, u], rm.at[2, u], c_send.at[0], rm_sem.at[2, u], xp)
        wait(rp.at[0, u], rp_sem.at[0, u])
        am[0, u] = (am[0, u].astype(F32) + rp[0, u].astype(F32)).astype(BF16)
        send(am.at[0, u], rp.at[2, u], c_send.at[1], rp_sem.at[2, u], xm)
        return carry

    lax.fori_loop(0, NA, direct, 0)

    def back(n, carry):
        nrow = pl.ds(pl.multiple_of(n * 256, 256), 256)
        dims = (((1,), (1,)), ((), ()))
        v = jnp.zeros((SLOTS, 256), F32)
        for i in range(6):
            w = wbuf[i // 3, nrow, pl.ds((i % 3) * BW, BW)]
            v = v + lax.dot_general(acts[i], w, dims, preferred_element_type=F32)
        rg[:, nrow] = v.astype(BF16)
        return carry

    lax.fori_loop(0, D // 256, back, 0)
    for i, b in enumerate(BLOCKS):
        rows = pl.ds(i * CAP, CAP)
        if b == (0, 0, 0):
            local(rg.at[rows], ret.at[rows], ret_sem)
        else:
            send(rg.at[rows], ret.at[rows], ret_send, ret_sem, near(*b))

    lax.fori_loop(0, NA, combine, 0)
    lax.fori_loop(NA, 2 * NA, direct, 0)
    lax.fori_loop(NA, 2 * NA, combine, 0)

    def own(u, carry):
        put(a0, u, product(0, u // NA, lax.rem(u, NA)))
        return carry

    lax.fori_loop(0, 2 * NA, own, 0)

    wait(yb_recv, yb_sem)

    def y_first(n, carry):
        u = 2 * NA + n
        put(a2, u, product(2, 1, NA + n) + yb_recv[2, n].astype(F32))
        send_far(u)
        put(ap, u, product(1, 1, NA + n) + yb_recv[1, n].astype(F32))
        put(am, u, product(3, 1, NA + n) + yb_recv[3, n].astype(F32))
        return carry

    lax.fori_loop(0, NB, y_first, 0)
    lax.fori_loop(2 * NA, NU, direct, 0)

    def y_own(n, carry):
        put(a0, 2 * NA + n, product(0, 1, NA + n) + yb_recv[0, n].astype(F32))
        return carry

    lax.fori_loop(0, NB, y_own, 0)

    def total(u, h):
        s = a0[h, u].astype(F32) + rp[2 - h, u].astype(F32)
        return s + rm[1 + h, u].astype(F32)

    def arrived(u):
        for i in (1, 2):
            wait(rp.at[i, u], rp_sem.at[i, u])
            wait(rm.at[i, u], rm_sem.at[i, u])

    def across(u, carry):
        arrived(u)
        for h in range(2):
            ysend[u, h] = total(u, h).astype(BF16)
        send(ysend.at[u], yrecv.at[u], y_send, y_sem.at[u], yo)
        return carry

    lax.fori_loop(0, NA, across, 0)
    lax.fori_loop(2 * NA, NU, combine, 0)

    lane = lax.broadcasted_iota(jnp.int32, (1, SLOTS), 1)
    blk = lane // CAP
    expert = jnp.zeros((1, SLOTS), F32)
    for i, (dy, dz, dc) in enumerate(BLOCKS):
        expert = jnp.where(blk == i, exp_of(dy, -dz, dc).astype(F32), expert)
    slot = (lane - blk * CAP).astype(F32)
    ids_col = jnp.concatenate([mine_meta[...]] * (TOK // 8), axis=0).T
    h0 = jnp.where(ids_col[:, 0:1] == expert, 1.0, 0.0)
    h1 = jnp.where(ids_col[:, 1:2] == expert, 1.0, 0.0)
    after = jnp.where(row_i > col_i, 1.0, 0.0).astype(BF16)
    pos = jnp.dot(after, (h0 + h1).astype(BF16), preferred_element_type=F32)
    h0 = jnp.where(pos == slot, h0, 0.0).astype(BF16)
    h1 = jnp.where(pos == slot, h1, 0.0).astype(BF16)
    both = h0 + h1
    wait(ret, ret_sem)

    def gather(n, carry):
        ncol = pl.ds(pl.multiple_of(n * 256, 256), 256)
        ig_out[:, ncol] = jnp.dot(both, ret[:, ncol], preferred_element_type=F32).astype(BF16)
        return carry

    lax.fori_loop(0, D // 256, gather, 0)
    g = ret[:, pl.ds(D, TOK)]
    g0 = jnp.dot(h0, g, preferred_element_type=F32).T
    g1 = jnp.dot(h1, g, preferred_element_type=F32).T
    gg_out[...] = jnp.concatenate([g0[0:1], g1[0:1]], axis=0).astype(BF16)

    def finish(n, carry):
        u = NA + n
        arrived(u)
        wait(yrecv.at[n], y_sem.at[n])
        for h in range(2):
            s = total(u, h) + yrecv[n, h].astype(F32)
            dl_out[n, pl.ds(h * TOK, TOK), :] = (s * 0.125).astype(BF16)
        return carry

    lax.fori_loop(0, NA, finish, 0)

    def finish_y(n, carry):
        u = 2 * NA + n
        arrived(u)
        for h in range(2):
            dl_out[NA + n, pl.ds(h * TOK, TOK), :] = (total(u, h) * 0.125).astype(BF16)
        return carry

    lax.fori_loop(0, NB, finish_y, 0)

    for i in range(4):
        wait(mine_meta, m_send.at[i])
    wait(stg1.at[pl.ds(1, 3)], st_send.at[0])
    wait(stg2.at[pl.ds(1, 3)], st_send.at[1])
    wait(stg3, st_send.at[2])
    wait(stg4, st_send.at[3])
    wait(gs1.at[pl.ds(1, 3)], gsend.at[0])
    wait(gs2.at[pl.ds(1, 3)], gsend.at[1])
    wait(gs3, gsend.at[2])
    wait(gs4, gsend.at[3])
    for i in range(2):
        wait(a2.at[i], a2_send.at[i])
        wait(ap.at[i], d_send.at[i])
        wait(ap.at[i], c_send.at[i])
    wait(yb_send, yb_ssem)
    wait(ysend, y_send)
    wait(rg.at[pl.ds(CAP, SLOTS - CAP)], ret_send)


def place(ig, gg, dl, ig_out, gg_out, dg_out, du_out, dd_out):
    ig_out[...] = ig[...]
    gg_out[...] = gg[...]
    for n in range(FF // BW):
        cols = pl.ds(n * BW, BW)
        for m, ref in enumerate((dg_out, du_out, dd_out)):
            ref[0, :, cols] = dl[3 * m + n]


def on_device(features, out_grad, expert_ids, gate_probs, w_gate, w_up, w_down):
    vm, anyspace = pl.BlockSpec(memory_space=pltpu.VMEM), pl.BlockSpec(memory_space=pl.ANY)
    dma = pltpu.SemaphoreType.DMA
    ig, gg, dl = pl.pallas_call(
        kernel,
        name="moe",
        out_shape=(
            jax.ShapeDtypeStruct((TOK, D), BF16),
            jax.ShapeDtypeStruct((2, TOK), BF16),
            jax.ShapeDtypeStruct((9, 256, BW), BF16),
        ),
        in_specs=[anyspace, anyspace, vm, vm, anyspace, anyspace, anyspace],
        out_specs=(vm, vm, vm),
        scratch_shapes=[
            pltpu.VMEM((5, NCH, TOK, 2 * CW), BF16),
            pltpu.VMEM((8, TOK), F32),
            pltpu.VMEM((4, 8, TOK), F32),
            pltpu.VMEM((3, 64, TOK), BF16),
            pltpu.VMEM((2, 160, TOK), BF16),
            pltpu.VMEM((4, NCH, 48, 2 * CW), BF16),
            pltpu.VMEM((4, NCH, 32, 2 * CW), BF16),
            pltpu.VMEM((2, 4, NCH, CAP, 2 * CW), BF16),
            pltpu.VMEM((2, 2, NCH, CAP, 2 * CW), BF16),
            pltpu.VMEM((4, 48, TOK), BF16),
            pltpu.VMEM((4, 32, TOK), BF16),
            pltpu.VMEM((2, 4, CAP, TOK), BF16),
            pltpu.VMEM((2, 2, CAP, TOK), BF16),
            pltpu.VMEM((NCH, SLOTS, 2 * CW), BF16),
            pltpu.VMEM((SLOTS, TOK), BF16),
            pltpu.VMEM((3, D, FF), BF16),
            pltpu.VMEM((3, SLOTS, FF), F32),
            pltpu.VMEM((9, SLOTS, BW), BF16),
            pltpu.VMEM((SLOTS, D + TOK), BF16),
            pltpu.VMEM((SLOTS, D + TOK), BF16),
            pltpu.VMEM((2, NU, TOK, BW), BF16),
            pltpu.VMEM((2, NU, TOK, BW), BF16),
            pltpu.VMEM((2, NU, TOK, BW), BF16),
            pltpu.VMEM((2, NU, TOK, BW), BF16),
            pltpu.VMEM((3, NU, TOK, BW), BF16),
            pltpu.VMEM((3, NU, TOK, BW), BF16),
            pltpu.VMEM((4, NB, 256, BW), BF16),
            pltpu.VMEM((4, NB, 256, BW), BF16),
            pltpu.VMEM((NA, 2, TOK, BW), BF16),
            pltpu.VMEM((NA, 2, TOK, BW), BF16),
            dma((NCH,)),
            dma((3,)),
            dma((4,)),
            dma((4,)),
            dma((4,)),
            dma((2, NCH)),
            dma((2, NCH)),
            dma((4,)),
            dma((NCH,)),
            dma((NCH,)),
            dma((4,)),
            dma((2,)),
            dma((2,)),
            dma((2,)),
            dma((2,)),
            dma((3, NU)),
            dma((3, NU)),
            dma,
            dma,
            dma,
            dma((NA,)),
            dma,
            dma,
            pltpu.SemaphoreType.REGULAR((4,)),
        ],
        compiler_params=pltpu.CompilerParams(
            collective_id=0, has_side_effects=True, vmem_limit_bytes=67_000_000
        ),
    )(features, out_grad, expert_ids.T, gate_probs.T, w_gate, w_up, w_down)
    delta = jax.ShapeDtypeStruct((1, 256, FF), BF16)
    ig, gg, d_gate, d_up, d_down = pl.pallas_call(
        place,
        name="place",
        out_shape=(
            jax.ShapeDtypeStruct((TOK, D), BF16),
            jax.ShapeDtypeStruct((2, TOK), BF16),
            delta,
            delta,
            delta,
        ),
        in_specs=[vm] * 3,
        out_specs=(vm,) * 5,
    )(ig, gg, dl)
    return (ig, gg.T, d_gate, d_up, d_down)


def solution(mesh):
    rows = P(("rep", "exp"), None)
    weights = P("exp", None, None)
    deltas = P("exp", "rep", None)
    return jax.shard_map(
        on_device,
        mesh=mesh,
        in_specs=(rows, rows, rows, rows, weights, weights, weights),
        out_specs=(rows, rows, deltas, deltas, deltas),
        check_vma=False,
    )
```

```python
import functools

import jax
import jax.numpy as jnp
from jax import lax
from jax.experimental import pallas as pl
from jax.experimental.pallas import tpu as pltpu
from jax.sharding import PartitionSpec as P

MESH = pl.DeviceIdType.MESH
F32 = jnp.float32
BF16 = jnp.bfloat16
TOK = 128
D = 2048
FF = 768
CAP = 16
AHEAD = 4
NCH = 8
CW = D // NCH
SLOTS = 512
NEAR = 320
BW = 256
NA = 6
U0 = 6
NU = U0 + 2 * NA
QS = ((0, 0), (0, 1), (1, 0), (1, 1))
BLOCKS = tuple(
    [(dy, dz, dc) for dy, dc in QS for dz in (0, -1, 1, -2, 2)]
    + [(dy, -3, dc) for dy, dc in QS]
    + [(dy, 3, dc) for dy, dc in QS]
    + [(0, 4, dc) for dc in (0, 1)]
    + [(1, 4, dc) for dc in (0, 1)]
)


def kernel(
    feat, og, ids_row, gates_row, wg, wu, wd,
    ig_hbm, gg_hbm, dl_hbm,
    ig_out, gg_out, dl_out, out_sem,
    src, mine_meta, msrc, s1, s2, stg1, stg2, stg3, stg4, gs1, gs2, gs3, gs4, rbuf, gbuf,
    wbuf, acc, acts, xt, rg, ret, aa, rp, rm, ysend, yrecv,
    load_sem, w_sem, m_send, m_recv, ring_send, r1, r2, st_send, rx, rx2, gsend, grecv,
    a2_send, d_send, c_send, far_sem, in_sem, y_send, y_sem, ret_send, ret_sem, hop_sem,
):
    rep = lax.axis_index("rep")
    exp = lax.axis_index("exp")
    x = lax.rem(rep, 4)
    yh = rep // 4
    yl = exp // 16
    z = lax.rem(exp // 2, 8)
    c = lax.rem(exp, 2)

    def exp_of(dy, dz, dc):
        return lax.rem(yl + dy, 2) * 16 + lax.rem(z + dz + 8, 8) * 2 + lax.rem(c + dc, 2)

    def near(dy, dz, dc):
        return {"rep": rep, "exp": exp_of(dy, dz, dc)}

    xp = {"rep": yh * 4 + lax.rem(x + 1, 4), "exp": exp}
    xm = {"rep": yh * 4 + lax.rem(x + 3, 4), "exp": exp}
    yo = {"rep": (1 - yh) * 4 + x, "exp": exp}

    def send(a, b, ss, rs, to):
        pltpu.make_async_remote_copy(
            src_ref=a, dst_ref=b, send_sem=ss, recv_sem=rs, device_id=to, device_id_type=MESH
        ).start()

    def local(a, b, sem):
        pltpu.make_async_copy(a, b, sem).start()

    def wait(ref, sem):
        pltpu.make_async_copy(ref, ref, sem).wait()

    def place_of(half, role):
        return lax.rem(yh + 1 + half, 2) * 4 + lax.rem(x + 2 + 3 * role + 3 * (role * (role - 1) // 2), 4)

    def block_of(p):
        return place_of(p // 4, lax.rem(p, 4))

    for k in range(NCH):
        local(feat.at[:, pl.ds(k * CW, CW)], src.at[0, k], load_sem.at[min(k, 1)])
    for k in range(NCH):
        cols = pl.ds(pl.multiple_of(block_of(k) * CW, CW), CW)
        local(og.at[:, cols], src.at[0, NCH + k], load_sem.at[2])
    for m, w in enumerate((wg, wu, wd)):
        local(w.at[0], wbuf.at[m], w_sem.at[m])

    mine_meta[...] = jnp.zeros_like(mine_meta)
    mine_meta[0:2, :] = ids_row[...].astype(F32)
    mine_meta[2:4, :] = gates_row[...].astype(F32)

    up, down = near(0, 1, 0), near(0, -1, 0)
    barrier = pltpu.get_barrier_semaphore()
    peers = [up, down] + [near(dy, 0, dc) for dy, dc in QS[1:]] + [xp, xm, yo]
    for p in peers:
        pl.semaphore_signal(barrier, inc=1, device_id=p, device_id_type=MESH)
    pl.semaphore_wait(barrier, len(peers))

    send(mine_meta, msrc.at[0], m_send.at[0], m_recv.at[0], up)
    send(mine_meta, msrc.at[1], m_send.at[1], m_recv.at[1], down)
    def own_out(k):
        send(src.at[0, k], src.at[1, k], ring_send.at[0], r1.at[k], up)
        send(src.at[0, k], src.at[2, k], ring_send.at[1], r1.at[k], down)

    wait(src.at[0, 0], load_sem.at[0])
    own_out(0)
    wait(src.at[0, pl.ds(1, NCH - 1)], load_sem.at[1])
    for k in range(1, NCH):
        own_out(k)
    wait(src.at[0, pl.ds(NCH, NCH)], load_sem.at[2])

    def greet(i):
        for p in (up, down):
            pl.semaphore_signal(hop_sem.at[i], inc=1, device_id=p, device_id_type=MESH)

    def greeted(i):
        pl.semaphore_wait(hop_sem.at[i], 2)

    greet(0)
    row_i = lax.broadcasted_iota(jnp.int32, (TOK, TOK), 0)
    col_i = lax.broadcasted_iota(jnp.int32, (TOK, TOK), 1)
    before = jnp.where(row_i < col_i, 1.0, 0.0).astype(BF16)
    slot_i = lax.broadcasted_iota(jnp.int32, (CAP, TOK), 0).astype(F32)

    def pick(meta_v, experts):
        i0, i1, g0, g1 = [jnp.broadcast_to(meta_v[i : i + 1, :], (CAP, TOK)) for i in range(4)]
        rows, gates = [], []
        for e in experts:
            ef = e.astype(F32)
            m0, m1 = i0 == ef, i1 == ef
            hit = jnp.where(m0 | m1, 1.0, 0.0)
            pos = jnp.dot(hit.astype(BF16), before, preferred_element_type=F32)
            one = jnp.where(pos == slot_i, hit, 0.0)
            gate = jnp.sum(one * jnp.where(m0, g0, jnp.where(m1, g1, 0.0)), axis=1, keepdims=True)
            rows.append(one.astype(BF16))
            gates.append(jnp.broadcast_to(gate, (CAP, TOK)).astype(BF16))
        return rows, gates

    own_plane = [exp_of(dy, 0, dc) for dy, dc in QS]

    def plan_first(s, meta_v):
        rows, gates = pick(meta_v, own_plane)
        for q in range(4):
            s1[s, pl.ds(q * CAP, CAP), :] = rows[q]
            gs1[q, pl.ds(s * CAP, CAP), :] = gates[q]

    plan_first(0, mine_meta[...])
    wait(msrc.at[0], m_recv.at[0])
    send(msrc.at[0], msrc.at[2], m_send.at[2], m_recv.at[2], up)
    wait(msrc.at[1], m_recv.at[1])
    send(msrc.at[1], msrc.at[3], m_send.at[3], m_recv.at[3], down)
    plan_first(1, msrc[0])
    plan_first(2, msrc[1])
    local(gs1.at[0], gbuf.at[pl.ds(0, 48)], grecv.at[0])
    for q in range(1, 4):
        send(gs1.at[q], gbuf.at[pl.ds(q * 80, 48)], gsend.at[0], grecv.at[0], near(QS[q][0], 0, QS[q][1]))

    def first(k):
        wait(src.at[pl.ds(1, 2), k], r1.at[k])
        send(src.at[1, k], src.at[3, k], ring_send.at[2], r2.at[k], up)
        send(src.at[2, k], src.at[4, k], ring_send.at[3], r2.at[k], down)
        for s in range(3):
            got = jnp.dot(s1[s], src[s, k], preferred_element_type=F32).astype(BF16)
            for q in range(4):
                stg1[q, k, pl.ds(s * CAP, CAP), :] = got[q * CAP : (q + 1) * CAP]
        local(stg1.at[0, k], rbuf.at[k, pl.ds(0, 48)], rx.at[k])
        for q in range(1, 4):
            send(stg1.at[q, k], rbuf.at[k, pl.ds(q * 80, 48)], st_send.at[0], rx.at[k], near(QS[q][0], 0, QS[q][1]))

    def first_x(k, carry):
        first(k)
        return carry

    for i in range(4):
        lax.fori_loop(2 * i, 2 * i + 2, first_x, 0)
        greeted(i)
        if i < 3:
            greet(i + 1)

    for d in range(2):
        step = 1 if d == 0 else -1
        wait(msrc.at[2 + d], m_recv.at[2 + d])
        third = [exp_of(dy, step, dc) for dy, dc in QS]
        fourth = [exp_of(d, 2 * step, dc) for dc in (0, 1)]
        rows, gates = pick(msrc[2 + d], own_plane + third + fourth)
        for i in range(10):
            s2[d, pl.ds(i * CAP, CAP), :] = rows[i]
        for q in range(4):
            gs2[q, pl.ds(d * CAP, CAP), :] = gates[q]
            gs3[d, q] = gates[4 + q]
        for i in range(2):
            gs4[d, i] = gates[8 + i]
    local(gs2.at[0], gbuf.at[pl.ds(48, 32)], grecv.at[0])
    for q in range(1, 4):
        send(gs2.at[q], gbuf.at[pl.ds(q * 80 + 48, 32)], gsend.at[1], grecv.at[0], near(QS[q][0], 0, QS[q][1]))
    for d in range(2):
        step = 1 if d == 0 else -1
        for q in range(4):
            send(gs3.at[d, q], gbuf.at[pl.ds(320 + (d * 4 + q) * CAP, CAP)], gsend.at[2], grecv.at[1], near(QS[q][0], step, QS[q][1]))
        for i in range(2):
            send(gs4.at[d, i], gbuf.at[pl.ds(448 + (d * 2 + i) * CAP, CAP)], gsend.at[3], grecv.at[1], near(d, 2 * step, i))

    def second(k):
        wait(src.at[pl.ds(3, 2), k], r2.at[k])
        for d in range(2):
            step = 1 if d == 0 else -1
            got = jnp.dot(s2[d], src[3 + d, k], preferred_element_type=F32).astype(BF16)
            for q in range(4):
                stg3[d, q, k] = got[(4 + q) * CAP : (5 + q) * CAP]
                stg2[q, k, pl.ds(d * CAP, CAP), :] = got[q * CAP : (q + 1) * CAP]
            for i in range(2):
                stg4[d, i, k] = got[(8 + i) * CAP : (9 + i) * CAP]
        local(stg2.at[0, k], rbuf.at[k, pl.ds(48, 32)], rx.at[k])
        for q in range(1, 4):
            send(stg2.at[q, k], rbuf.at[k, pl.ds(q * 80 + 48, 32)], st_send.at[1], rx.at[k], near(QS[q][0], 0, QS[q][1]))
        for d in range(2):
            step = 1 if d == 0 else -1
            for i in range(2):
                send(stg4.at[d, i, k], rbuf.at[k, pl.ds(448 + (d * 2 + i) * CAP, CAP)], st_send.at[3], rx2.at[k], near(d, 2 * step, i))
            for q in range(4):
                send(stg3.at[d, q, k], rbuf.at[k, pl.ds(320 + (d * 4 + q) * CAP, CAP)], st_send.at[2], rx2.at[k], near(QS[q][0], step, QS[q][1]))

    def second_x(k, carry):
        second(k)
        return carry

    lax.fori_loop(0, NCH, second_x, 0)
    for k in range(AHEAD):
        own_out(NCH + k)

    for m in range(3):
        wait(wbuf.at[m], w_sem.at[m])
    for k in range(NCH):
        wait(rbuf.at[k, pl.ds(0, NEAR)], rx.at[k])

    def near_x(n, carry):
        ncol = pl.ds(pl.multiple_of(n * 256, 256), 256)
        for m in range(2):
            v = jnp.zeros((NEAR, 256), F32)
            for k in range(NCH):
                v = v + jnp.dot(
                    rbuf[k, pl.ds(0, NEAR), :], wbuf[m, pl.ds(k * CW, CW), ncol], preferred_element_type=F32
                )
            acc[m, pl.ds(0, NEAR), ncol] = v
        return carry

    lax.fori_loop(0, FF // 256, near_x, 0)

    def turn_x(k, carry):
        xt[0, k, :, pl.ds(0, 256)] = rbuf[k, pl.ds(0, 256), :].T
        return carry

    lax.fori_loop(0, NCH, turn_x, 0)

    def hidden(i, carry):
        rows = pl.ds(pl.multiple_of(i * 32, 32), 32)
        pg, pu = acc[0, rows, :], acc[1, rows, :]
        sig = jax.nn.sigmoid(pg)
        act = pg * sig
        acts[2, rows, :] = (act * pu).astype(BF16)
        acc[0, rows, :] = pu * sig * (1.0 + pg * (1.0 - sig))
        acc[1, rows, :] = act
        return carry

    lax.fori_loop(0, NEAR // 32, hidden, 0)

    rest = pl.ds(NEAR, SLOTS - NEAR)

    def add_to(m, rows, first_one, part):
        @pl.when(first_one)
        def _():
            acc[m, rows, :] = part

        @pl.when(jnp.logical_not(first_one))
        def _():
            acc[m, rows, :] = acc[m, rows, :] + part

    def far_x(k, carry):
        wait(rbuf.at[k, rest], rx2.at[k])
        krow = pl.ds(pl.multiple_of(k * CW, CW), CW)
        for m in range(2):
            add_to(m, rest, k == 0, jnp.dot(rbuf[k, rest, :], wbuf[m, krow, :], preferred_element_type=F32))
        xt[0, k, :, pl.ds(256, 256)] = rbuf[k, pl.ds(256, 256), :].T
        return carry

    lax.fori_loop(0, NCH // 2, far_x, 0)
    first(NCH)
    first(NCH + 1)
    lax.fori_loop(NCH // 2, NCH, far_x, 0)
    lax.fori_loop(NEAR // 32, SLOTS // 32, hidden, 0)

    def product(role, half, m, cols=slice(None)):
        return jnp.dot(xt[m // 2, place_of(half, role)], acts[m, :, cols], preferred_element_type=F32)

    def put(role, u, v):
        v = v.astype(BF16)
        for i in range(v.shape[1] // BW):
            aa[role, 0, u + i] = v[:TOK, i * BW : (i + 1) * BW]
            aa[role, 1, u + i] = v[TOK:, i * BW : (i + 1) * BW]

    def send_far(u):
        send(aa.at[0, 0, u], rp.at[0, u], a2_send.at[0], far_sem.at[u], xm)
        send(aa.at[0, 1, u], rm.at[0, u], a2_send.at[1], far_sem.at[u], xp)

    def direct_up(u):
        send(aa.at[1, 0, u], rm.at[1, u], d_send.at[0], in_sem.at[u], xp)

    def direct_down(u):
        send(aa.at[2, 1, u], rp.at[1, u], d_send.at[1], in_sem.at[u], xm)

    def direct(u, carry):
        direct_up(u)
        direct_down(u)
        return carry

    def combine(u, carry):
        wait(aa.at[pl.ds(0, 2), 0, u], far_sem.at[u])
        aa[1, 1, u] = (aa[1, 1, u].astype(F32) + rm[0, u].astype(F32)).astype(BF16)
        send(aa.at[1, 1, u], rm.at[2, u], c_send.at[0], in_sem.at[u], xp)
        aa[2, 0, u] = (aa[2, 0, u].astype(F32) + rp[0, u].astype(F32)).astype(BF16)
        send(aa.at[2, 0, u], rp.at[2, u], c_send.at[1], in_sem.at[u], xm)
        return carry

    wait(gbuf.at[pl.ds(0, NEAR)], grecv.at[0])
    wait(gbuf.at[rest], grecv.at[1])

    def turn_dy(p, r0):
        rows = pl.ds(r0, 256)
        g = gbuf[rows, :].astype(F32)
        g = jnp.concatenate([g, g], axis=1)
        xt[1, block_of(p), :, rows] = (g * rbuf[NCH + p, rows, :].astype(F32)).astype(BF16).T

    def down_rows(p):
        return pl.ds(pl.multiple_of(block_of(p) * CW, CW), CW)

    def dy_near(p):
        k = NCH + p
        rows = pl.ds(0, NEAR)
        wait(rbuf.at[k, rows], rx.at[k])
        add_to(2, rows, p == 0, jnp.dot(rbuf[k, rows, :], wbuf[2, down_rows(p), :], preferred_element_type=F32))
        turn_dy(p, 0)

    def dy_far(p):
        k = NCH + p
        wait(rbuf.at[k, rest], rx2.at[k])
        add_to(2, rest, p == 0, jnp.dot(rbuf[k, rest, :], wbuf[2, down_rows(p), :], preferred_element_type=F32))
        turn_dy(p, 256)

    def dy_gradient(p):
        half, role = p // 4, lax.rem(p, 4)
        put(role, half * 3, product(role, half, 2))
        for i in range(3):
            u = half * 3 + i

            @pl.when(role == 0)
            def _():
                send_far(u)

            @pl.when(role == 1)
            def _():
                direct_up(u)

            @pl.when(role == 2)
            def _():
                direct_down(u)

        @pl.when(role == 2)
        def _():
            for i in range(3):
                combine(half * 3 + i, 0)

    def cotangents(j, carry):
        @pl.when(j + AHEAD < NCH)
        def _():
            own_out(NCH + AHEAD + j)

        @pl.when(j + 2 < NCH)
        def _():
            first(NCH + 2 + j)

        second(NCH + j)

        @pl.when(j >= 1)
        def _():
            dy_near(j - 1)

        @pl.when(j >= 2)
        def _():
            dy_far(j - 2)
            dy_gradient(j - 2)

        return carry

    lax.fori_loop(0, NCH, cotangents, 0)

    def pointwise(i, carry):
        rows = pl.ds(pl.multiple_of(i * 32, 32), 32)
        g = gbuf[rows, pl.ds(0, 1)].astype(F32)
        bg = acc[2, rows, :]
        gate = jnp.sum(bg * acts[2, rows, :].astype(F32), axis=1, keepdims=True)
        dh = g * bg
        acts[0, rows, :] = (dh * acc[0, rows, :]).astype(BF16)
        acts[1, rows, :] = (dh * acc[1, rows, :]).astype(BF16)
        rg[rows, pl.ds(D, TOK)] = jnp.broadcast_to(gate, (32, TOK)).astype(BF16)
        return carry

    def back(rows, n):
        nrow = pl.ds(pl.multiple_of(n * 256, 256), 256)
        dims = (((1,), (1,)), ((), ()))
        v = jnp.zeros((rows.size, 256), F32)
        for m in range(2):
            v = v + lax.dot_general(acts[m, rows, :], wbuf[m, nrow, :], dims, preferred_element_type=F32)
        rg[rows, nrow] = v.astype(BF16)

    def back_near(n, carry):
        back(pl.ds(0, NEAR), n)
        return carry

    def back_far(n, carry):
        back(rest, n)
        return carry

    def give_back(lo, hi, dy):
        for i in range(lo, hi):
            rows = pl.ds(i * CAP, CAP)
            if BLOCKS[i] == (0, 0, 0) and dy == 0:
                local(rg.at[rows], ret.at[rows], ret_sem)
            elif BLOCKS[i][0] == dy:
                send(rg.at[rows], ret.at[rows], ret_send, ret_sem, near(*BLOCKS[i]))

    dy_near(NCH - 1)
    lax.fori_loop(0, NEAR // 32, pointwise, 0)
    dy_far(NCH - 2)
    dy_far(NCH - 1)
    lax.fori_loop(NEAR // 32, SLOTS // 32, pointwise, 0)

    def gate_up(role, half):
        u = U0 + half * NA
        put(role, u, product(role, half, 0))
        put(role, u + 3, product(role, half, 1))

    def far_units(half, carry):
        gate_up(0, half)
        for i in range(NA):
            send_far(U0 + half * NA + i)
        return carry

    def beside(half, carry):
        for role in (1, 2):
            gate_up(role, half)
        return carry

    def own(half, carry):
        gate_up(3, half)
        return carry

    def total(u, h):
        s = aa[3, h, u].astype(F32) + rp[2 - h, u].astype(F32)
        return s + rm[1 + h, u].astype(F32)

    def arrived(u):
        wait(aa.at[:, 0, u], in_sem.at[u])

    def across(v, u):
        arrived(u)
        for h in range(2):
            ysend[v, h] = total(u, h).astype(BF16)
        send(ysend.at[v], yrecv.at[v], y_send, y_sem.at[v], yo)

    def across_down(i, carry):
        across(i, i)
        return carry


    def across_rest(i, carry):
        across(3 + i, U0 + i)
        return carry

    lax.fori_loop(0, 1, far_units, 0)
    lax.fori_loop(0, 3, across_down, 0)
    dy_gradient(NCH - 2)
    lax.fori_loop(0, D // 256, back_near, 0)
    give_back(0, NEAR // CAP, 1)
    lax.fori_loop(0, D // 256, back_far, 0)
    give_back(NEAR // CAP, SLOTS // CAP, 1)
    give_back(NEAR // CAP, SLOTS // CAP, 0)
    give_back(0, NEAR // CAP, 0)
    lax.fori_loop(0, 1, beside, 0)
    dy_gradient(NCH - 1)
    lax.fori_loop(U0, U0 + NA, direct, 0)
    lax.fori_loop(U0, U0 + NA, combine, 0)
    lax.fori_loop(1, 2, far_units, 0)
    lax.fori_loop(1, 2, beside, 0)
    lax.fori_loop(U0 + NA, NU, direct, 0)
    lax.fori_loop(0, 2, own, 0)
    lax.fori_loop(0, NA, across_rest, 0)
    lax.fori_loop(U0 + NA, NU, combine, 0)

    lane = lax.broadcasted_iota(jnp.int32, (1, SLOTS), 1)
    blk = lane // CAP
    expert = jnp.zeros((1, SLOTS), F32)
    for i, (dy, dz, dc) in enumerate(BLOCKS):
        expert = jnp.where(blk == i, exp_of(dy, -dz, dc).astype(F32), expert)
    slot = (lane - blk * CAP).astype(F32)
    ids_col = jnp.concatenate([mine_meta[...]] * (TOK // 8), axis=0).T
    h0 = jnp.where(ids_col[:, 0:1] == expert, 1.0, 0.0)
    h1 = jnp.where(ids_col[:, 1:2] == expert, 1.0, 0.0)
    after = jnp.where(row_i > col_i, 1.0, 0.0).astype(BF16)
    pos = jnp.dot(after, (h0 + h1).astype(BF16), preferred_element_type=F32)
    h0 = jnp.where(pos == slot, h0, 0.0).astype(BF16)
    h1 = jnp.where(pos == slot, h1, 0.0).astype(BF16)
    both = h0 + h1
    wait(ret, ret_sem)

    def gather(n, carry):
        ncol = pl.ds(pl.multiple_of(n * 256, 256), 256)
        ig_out[:, ncol] = jnp.dot(both, ret[:, ncol], preferred_element_type=F32).astype(BF16)
        return carry

    lax.fori_loop(0, D // 256, gather, 0)
    local(ig_out, ig_hbm, out_sem.at[0])
    g = ret[:, pl.ds(D, TOK)]
    g0 = jnp.dot(h0, g, preferred_element_type=F32).T
    g1 = jnp.dot(h1, g, preferred_element_type=F32).T
    gg_out[...] = jnp.concatenate([g0[0:1], g1[0:1]], axis=0).astype(BF16)
    local(gg_out, gg_hbm, out_sem.at[1])

    def finish(n, v, u):
        arrived(u)
        wait(yrecv.at[v], y_sem.at[v])
        for h in range(2):
            s = total(u, h) + yrecv[v, h].astype(F32)
            dl_out[n, pl.ds(h * TOK, TOK), :] = (s * 0.125).astype(BF16)
        local(dl_out.at[n], dl_hbm.at[n], out_sem.at[2])

    def finish_down(i, carry):
        finish(6 + i, i, 3 + i)
        return carry

    def finish_rest(i, carry):
        finish(i, 3 + i, U0 + NA + i)
        return carry

    lax.fori_loop(0, 3, finish_down, 0)
    lax.fori_loop(0, NA, finish_rest, 0)

    for i in range(4):
        wait(mine_meta, m_send.at[i])
    wait(stg1.at[pl.ds(1, 3)], st_send.at[0])
    wait(stg2.at[pl.ds(1, 3)], st_send.at[1])
    wait(stg3, st_send.at[2])
    wait(stg4, st_send.at[3])
    wait(gs1.at[pl.ds(1, 3)], gsend.at[0])
    wait(gs2.at[pl.ds(1, 3)], gsend.at[1])
    wait(gs3, gsend.at[2])
    wait(gs4, gsend.at[3])
    for i in range(2):
        wait(src.at[0], ring_send.at[i])
        wait(src.at[1], ring_send.at[2 + i])
        wait(aa.at[0, i], a2_send.at[i])
        wait(aa.at[0, i], d_send.at[i])
        wait(aa.at[0, i], c_send.at[i])
    wait(ysend, y_send)
    wait(rg.at[pl.ds(CAP, SLOTS - CAP)], ret_send)
    wait(ig_out, out_sem.at[0])
    wait(gg_out, out_sem.at[1])
    wait(dl_out, out_sem.at[2])


def place(ig, gg, dl, ig_out, gg_out, dg_out, du_out, dd_out, ig_v, gg_v, dl_v, in_sem, out_sem):
    def copies(out):
        pairs = [(ig, ig_v, ig_out), (gg, gg_v, gg_out)]
        for n in range(9):
            to = (dg_out, du_out, dd_out)[n // 3].at[0, :, pl.ds((n % 3) * BW, BW)]
            pairs.append((dl.at[n], dl_v.at[n], to))
        if out:
            return [pltpu.make_async_copy(v, o, out_sem.at[i]) for i, (_, v, o) in enumerate(pairs)]
        return [pltpu.make_async_copy(a, v, in_sem.at[i]) for i, (a, v, _) in enumerate(pairs)]

    ins, outs = copies(False), copies(True)
    for c in ins:
        c.start()
    for a, b in zip(ins, outs):
        a.wait()
        b.start()
    for c in outs:
        c.wait()


def on_device(features, out_grad, expert_ids, gate_probs, w_gate, w_up, w_down):
    vm, anyspace = pl.BlockSpec(memory_space=pltpu.VMEM), pl.BlockSpec(memory_space=pl.ANY)
    dma = pltpu.SemaphoreType.DMA
    ig, gg, dl = pl.pallas_call(
        kernel,
        name="moe",
        out_shape=(
            jax.ShapeDtypeStruct((TOK, D), BF16),
            jax.ShapeDtypeStruct((2, TOK), BF16),
            jax.ShapeDtypeStruct((9, 256, BW), BF16),
        ),
        in_specs=[anyspace, anyspace, vm, vm, anyspace, anyspace, anyspace],
        out_specs=(anyspace, anyspace, anyspace),
        scratch_shapes=[
            pltpu.VMEM((TOK, D), BF16),
            pltpu.VMEM((2, TOK), BF16),
            pltpu.VMEM((9, 256, BW), BF16),
            dma((3,)),
            pltpu.VMEM((5, 2 * NCH, TOK, CW), BF16),
            pltpu.VMEM((8, TOK), F32),
            pltpu.VMEM((4, 8, TOK), F32),
            pltpu.VMEM((3, 64, TOK), BF16),
            pltpu.VMEM((2, 160, TOK), BF16),
            pltpu.VMEM((4, 2 * NCH, 48, CW), BF16),
            pltpu.VMEM((4, 2 * NCH, 32, CW), BF16),
            pltpu.VMEM((2, 4, 2 * NCH, CAP, CW), BF16),
            pltpu.VMEM((2, 2, 2 * NCH, CAP, CW), BF16),
            pltpu.VMEM((4, 48, TOK), BF16),
            pltpu.VMEM((4, 32, TOK), BF16),
            pltpu.VMEM((2, 4, CAP, TOK), BF16),
            pltpu.VMEM((2, 2, CAP, TOK), BF16),
            pltpu.VMEM((2 * NCH, SLOTS, CW), BF16),
            pltpu.VMEM((SLOTS, TOK), BF16),
            pltpu.VMEM((3, D, FF), BF16),
            pltpu.VMEM((3, SLOTS, FF), F32),
            pltpu.VMEM((3, SLOTS, FF), BF16),
            pltpu.VMEM((2, NCH, CW, SLOTS), BF16),
            pltpu.VMEM((SLOTS, D + TOK), BF16),
            pltpu.VMEM((SLOTS, D + TOK), BF16),
            pltpu.VMEM((4, 2, NU, TOK, BW), BF16),
            pltpu.VMEM((3, NU, TOK, BW), BF16),
            pltpu.VMEM((3, NU, TOK, BW), BF16),
            pltpu.VMEM((3 + NA, 2, TOK, BW), BF16),
            pltpu.VMEM((3 + NA, 2, TOK, BW), BF16),
            dma((3,)),
            dma((3,)),
            dma((4,)),
            dma((4,)),
            dma((4,)),
            dma((2 * NCH,)),
            dma((2 * NCH,)),
            dma((4,)),
            dma((2 * NCH,)),
            dma((2 * NCH,)),
            dma((4,)),
            dma((2,)),
            dma((2,)),
            dma((2,)),
            dma((2,)),
            dma((NU,)),
            dma((NU,)),
            dma,
            dma((3 + NA,)),
            dma,
            dma,
            pltpu.SemaphoreType.REGULAR((4,)),
        ],
        compiler_params=pltpu.CompilerParams(
            collective_id=0, has_side_effects=True, vmem_limit_bytes=67_000_000
        ),
    )(features, out_grad, expert_ids.T, gate_probs.T, w_gate, w_up, w_down)
    delta = jax.ShapeDtypeStruct((1, 256, FF), BF16)
    ig, gg, d_gate, d_up, d_down = pl.pallas_call(
        place,
        name="place",
        out_shape=(
            jax.ShapeDtypeStruct((TOK, D), BF16),
            jax.ShapeDtypeStruct((2, TOK), BF16),
            delta,
            delta,
            delta,
        ),
        in_specs=[anyspace] * 3,
        out_specs=(anyspace,) * 5,
        scratch_shapes=[
            pltpu.VMEM((TOK, D), BF16),
            pltpu.VMEM((2, TOK), BF16),
            pltpu.VMEM((9, 256, BW), BF16),
            dma((11,)),
            dma((11,)),
        ],
    )(ig, gg, dl)
    return (ig, gg.T, d_gate, d_up, d_down)


def solution(mesh):
    rows = P(("rep", "exp"), None)
    weights = P("exp", None, None)
    deltas = P("exp", "rep", None)
    return jax.shard_map(
        on_device,
        mesh=mesh,
        in_specs=(rows, rows, rows, rows, weights, weights, weights),
        out_specs=(rows, rows, deltas, deltas, deltas),
        check_vma=False,
    )
```

```python
import functools

import jax
import jax.numpy as jnp
from jax import lax
from jax.experimental import pallas as pl
from jax.experimental.pallas import tpu as pltpu
from jax.sharding import PartitionSpec as P

MESH = pl.DeviceIdType.MESH
F32 = jnp.float32
BF16 = jnp.bfloat16
TOK = 128
D = 2048
FF = 768
CAP = 16
AHEAD = 4
NCH = 8
CW = D // NCH
SLOTS = 512
NEAR = 320
BW = 256
NA = 6
U0 = 6
NU = U0 + 2 * NA
QS = ((0, 0), (0, 1), (1, 0), (1, 1))
BLOCKS = tuple(
    [(dy, dz, dc) for dy, dc in QS for dz in (0, -1, 1, -2, 2)]
    + [(dy, -3, dc) for dy, dc in QS]
    + [(dy, 3, dc) for dy, dc in QS]
    + [(0, 4, dc) for dc in (0, 1)]
    + [(1, 4, dc) for dc in (0, 1)]
)


def kernel(
    feat, og, ids_row, gates_row, wg, wu, wd,
    ig_hbm, gg_hbm, dl_hbm,
    ig_out, gg_out, dl_out, out_sem,
    src, mine_meta, msrc, s1, s2, stg1, stg2, stg3, stg4, gs1, gs2, gs3, gs4, rbuf, gbuf,
    wbuf, acc, acts, xt, rg, ret, aa, rp, rm, ysend, yrecv,
    load_sem, w_sem, m_send, m_recv, ring_send, r1, r2, st_send, rx, rx2, gsend, grecv,
    a2_send, d_send, c_send, far_sem, in_sem, y_send, y_sem, ret_send, ret_sem, hop_sem,
):
    rep = lax.axis_index("rep")
    exp = lax.axis_index("exp")
    x = lax.rem(rep, 4)
    yh = rep // 4
    yl = exp // 16
    z = lax.rem(exp // 2, 8)
    c = lax.rem(exp, 2)

    def exp_of(dy, dz, dc):
        return lax.rem(yl + dy, 2) * 16 + lax.rem(z + dz + 8, 8) * 2 + lax.rem(c + dc, 2)

    def near(dy, dz, dc):
        return {"rep": rep, "exp": exp_of(dy, dz, dc)}

    xp = {"rep": yh * 4 + lax.rem(x + 1, 4), "exp": exp}
    xm = {"rep": yh * 4 + lax.rem(x + 3, 4), "exp": exp}
    yo = {"rep": (1 - yh) * 4 + x, "exp": exp}

    def send(a, b, ss, rs, to):
        pltpu.make_async_remote_copy(
            src_ref=a, dst_ref=b, send_sem=ss, recv_sem=rs, device_id=to, device_id_type=MESH
        ).start()

    def local(a, b, sem):
        pltpu.make_async_copy(a, b, sem).start()

    def wait(ref, sem):
        pltpu.make_async_copy(ref, ref, sem).wait()

    def place_of(half, role):
        return lax.rem(yh + 1 + half, 2) * 4 + lax.rem(x + 2 + 3 * role + 3 * (role * (role - 1) // 2), 4)

    def part_of(p):
        own = p // 6
        return own * (p - 6) + (1 - own) * (p // 3), own * 3 + (1 - own) * lax.rem(p, 3)

    def block_of(p):
        return place_of(*part_of(p))

    for k in range(NCH):
        local(feat.at[:, pl.ds(k * CW, CW)], src.at[0, k], load_sem.at[min(k, 1)])
    for k in range(NCH):
        cols = pl.ds(pl.multiple_of(block_of(k) * CW, CW), CW)
        local(og.at[:, cols], src.at[0, NCH + k], load_sem.at[2])
    for m, w in enumerate((wg, wu, wd)):
        local(w.at[0], wbuf.at[m], w_sem.at[m])

    mine_meta[...] = jnp.zeros_like(mine_meta)
    mine_meta[0:2, :] = ids_row[...].astype(F32)
    mine_meta[2:4, :] = gates_row[...].astype(F32)

    up, down = near(0, 1, 0), near(0, -1, 0)
    barrier = pltpu.get_barrier_semaphore()
    peers = [up, down] + [near(dy, 0, dc) for dy, dc in QS[1:]] + [xp, xm, yo]
    for p in peers:
        pl.semaphore_signal(barrier, inc=1, device_id=p, device_id_type=MESH)
    pl.semaphore_wait(barrier, len(peers))

    send(mine_meta, msrc.at[0], m_send.at[0], m_recv.at[0], up)
    send(mine_meta, msrc.at[1], m_send.at[1], m_recv.at[1], down)
    def own_out(k):
        send(src.at[0, k], src.at[1, k], ring_send.at[0], r1.at[k], up)
        send(src.at[0, k], src.at[2, k], ring_send.at[1], r1.at[k], down)

    wait(src.at[0, 0], load_sem.at[0])
    own_out(0)
    wait(src.at[0, pl.ds(1, NCH - 1)], load_sem.at[1])
    for k in range(1, NCH):
        own_out(k)
    wait(src.at[0, pl.ds(NCH, NCH)], load_sem.at[2])

    def greet(i):
        for p in (up, down):
            pl.semaphore_signal(hop_sem.at[i], inc=1, device_id=p, device_id_type=MESH)

    def greeted(i):
        pl.semaphore_wait(hop_sem.at[i], 2)

    greet(0)
    row_i = lax.broadcasted_iota(jnp.int32, (TOK, TOK), 0)
    col_i = lax.broadcasted_iota(jnp.int32, (TOK, TOK), 1)
    before = jnp.where(row_i < col_i, 1.0, 0.0).astype(BF16)
    slot_i = lax.broadcasted_iota(jnp.int32, (CAP, TOK), 0).astype(F32)

    def pick(meta_v, experts):
        i0, i1, g0, g1 = [jnp.broadcast_to(meta_v[i : i + 1, :], (CAP, TOK)) for i in range(4)]
        rows, gates = [], []
        for e in experts:
            ef = e.astype(F32)
            m0, m1 = i0 == ef, i1 == ef
            hit = jnp.where(m0 | m1, 1.0, 0.0)
            pos = jnp.dot(hit.astype(BF16), before, preferred_element_type=F32)
            one = jnp.where(pos == slot_i, hit, 0.0)
            gate = jnp.sum(one * jnp.where(m0, g0, jnp.where(m1, g1, 0.0)), axis=1, keepdims=True)
            rows.append(one.astype(BF16))
            gates.append(jnp.broadcast_to(gate, (CAP, TOK)).astype(BF16))
        return rows, gates

    own_plane = [exp_of(dy, 0, dc) for dy, dc in QS]

    def plan_first(s, meta_v):
        rows, gates = pick(meta_v, own_plane)
        for q in range(4):
            s1[s, pl.ds(q * CAP, CAP), :] = rows[q]
            gs1[q, pl.ds(s * CAP, CAP), :] = gates[q]

    plan_first(0, mine_meta[...])
    wait(msrc.at[0], m_recv.at[0])
    send(msrc.at[0], msrc.at[2], m_send.at[2], m_recv.at[2], up)
    wait(msrc.at[1], m_recv.at[1])
    send(msrc.at[1], msrc.at[3], m_send.at[3], m_recv.at[3], down)
    plan_first(1, msrc[0])
    plan_first(2, msrc[1])
    local(gs1.at[0], gbuf.at[pl.ds(0, 48)], grecv.at[0])
    for q in range(1, 4):
        send(gs1.at[q], gbuf.at[pl.ds(q * 80, 48)], gsend.at[0], grecv.at[0], near(QS[q][0], 0, QS[q][1]))

    def first(k):
        wait(src.at[pl.ds(1, 2), k], r1.at[k])
        send(src.at[1, k], src.at[3, k], ring_send.at[2], r2.at[k], up)
        send(src.at[2, k], src.at[4, k], ring_send.at[3], r2.at[k], down)
        for s in range(3):
            got = jnp.dot(s1[s], src[s, k], preferred_element_type=F32).astype(BF16)
            for q in range(4):
                stg1[q, k, pl.ds(s * CAP, CAP), :] = got[q * CAP : (q + 1) * CAP]
        local(stg1.at[0, k], rbuf.at[k, pl.ds(0, 48)], rx.at[k])
        for q in range(1, 4):
            send(stg1.at[q, k], rbuf.at[k, pl.ds(q * 80, 48)], st_send.at[0], rx.at[k], near(QS[q][0], 0, QS[q][1]))

    def first_x(k, carry):
        first(k)
        return carry

    for i in range(4):
        lax.fori_loop(2 * i, 2 * i + 2, first_x, 0)
        greeted(i)
        if i < 3:
            greet(i + 1)

    for d in range(2):
        step = 1 if d == 0 else -1
        wait(msrc.at[2 + d], m_recv.at[2 + d])
        third = [exp_of(dy, step, dc) for dy, dc in QS]
        fourth = [exp_of(d, 2 * step, dc) for dc in (0, 1)]
        rows, gates = pick(msrc[2 + d], own_plane + third + fourth)
        for i in range(10):
            s2[d, pl.ds(i * CAP, CAP), :] = rows[i]
        for q in range(4):
            gs2[q, pl.ds(d * CAP, CAP), :] = gates[q]
            gs3[d, q] = gates[4 + q]
        for i in range(2):
            gs4[d, i] = gates[8 + i]
    local(gs2.at[0], gbuf.at[pl.ds(48, 32)], grecv.at[0])
    for q in range(1, 4):
        send(gs2.at[q], gbuf.at[pl.ds(q * 80 + 48, 32)], gsend.at[1], grecv.at[0], near(QS[q][0], 0, QS[q][1]))
    for d in range(2):
        step = 1 if d == 0 else -1
        for q in range(4):
            send(gs3.at[d, q], gbuf.at[pl.ds(320 + (d * 4 + q) * CAP, CAP)], gsend.at[2], grecv.at[1], near(QS[q][0], step, QS[q][1]))
        for i in range(2):
            send(gs4.at[d, i], gbuf.at[pl.ds(448 + (d * 2 + i) * CAP, CAP)], gsend.at[3], grecv.at[1], near(d, 2 * step, i))

    def second(k):
        wait(src.at[pl.ds(3, 2), k], r2.at[k])
        for d in range(2):
            step = 1 if d == 0 else -1
            got = jnp.dot(s2[d], src[3 + d, k], preferred_element_type=F32).astype(BF16)
            for q in range(4):
                stg3[d, q, k] = got[(4 + q) * CAP : (5 + q) * CAP]
                stg2[q, k, pl.ds(d * CAP, CAP), :] = got[q * CAP : (q + 1) * CAP]
            for i in range(2):
                stg4[d, i, k] = got[(8 + i) * CAP : (9 + i) * CAP]
        local(stg2.at[0, k], rbuf.at[k, pl.ds(48, 32)], rx.at[k])
        for q in range(1, 4):
            send(stg2.at[q, k], rbuf.at[k, pl.ds(q * 80 + 48, 32)], st_send.at[1], rx.at[k], near(QS[q][0], 0, QS[q][1]))
        for d in range(2):
            step = 1 if d == 0 else -1
            for i in range(2):
                send(stg4.at[d, i, k], rbuf.at[k, pl.ds(448 + (d * 2 + i) * CAP, CAP)], st_send.at[3], rx2.at[k], near(d, 2 * step, i))
            for q in range(4):
                send(stg3.at[d, q, k], rbuf.at[k, pl.ds(320 + (d * 4 + q) * CAP, CAP)], st_send.at[2], rx2.at[k], near(QS[q][0], step, QS[q][1]))

    def second_x(k, carry):
        second(k)
        return carry

    lax.fori_loop(0, NCH, second_x, 0)
    for k in range(AHEAD):
        own_out(NCH + k)

    for m in range(3):
        wait(wbuf.at[m], w_sem.at[m])
    for k in range(NCH):
        wait(rbuf.at[k, pl.ds(0, NEAR)], rx.at[k])

    def near_x(n, carry):
        ncol = pl.ds(pl.multiple_of(n * 256, 256), 256)
        for m in range(2):
            v = jnp.zeros((NEAR, 256), F32)
            for k in range(NCH):
                v = v + jnp.dot(
                    rbuf[k, pl.ds(0, NEAR), :], wbuf[m, pl.ds(k * CW, CW), ncol], preferred_element_type=F32
                )
            acc[m, pl.ds(0, NEAR), ncol] = v
        return carry

    lax.fori_loop(0, FF // 256, near_x, 0)

    def turn_x(k, carry):
        xt[0, k, :, pl.ds(0, 256)] = rbuf[k, pl.ds(0, 256), :].T
        return carry

    lax.fori_loop(0, NCH, turn_x, 0)

    def hidden(i, carry):
        rows = pl.ds(pl.multiple_of(i * 32, 32), 32)
        pg, pu = acc[0, rows, :], acc[1, rows, :]
        sig = jax.nn.sigmoid(pg)
        act = pg * sig
        acts[2, rows, :] = (act * pu).astype(BF16)
        acc[0, rows, :] = pu * sig * (1.0 + pg * (1.0 - sig))
        acc[1, rows, :] = act
        return carry

    lax.fori_loop(0, NEAR // 32, hidden, 0)

    rest = pl.ds(NEAR, SLOTS - NEAR)

    def add_to(m, rows, first_one, part):
        @pl.when(first_one)
        def _():
            acc[m, rows, :] = part

        @pl.when(jnp.logical_not(first_one))
        def _():
            acc[m, rows, :] = acc[m, rows, :] + part

    def far_x(k, carry):
        wait(rbuf.at[k, rest], rx2.at[k])
        krow = pl.ds(pl.multiple_of(k * CW, CW), CW)
        for m in range(2):
            add_to(m, rest, k == 0, jnp.dot(rbuf[k, rest, :], wbuf[m, krow, :], preferred_element_type=F32))
        xt[0, k, :, pl.ds(256, 256)] = rbuf[k, pl.ds(256, 256), :].T
        return carry

    lax.fori_loop(0, NCH // 2, far_x, 0)
    first(NCH)
    first(NCH + 1)
    lax.fori_loop(NCH // 2, NCH, far_x, 0)
    lax.fori_loop(NEAR // 32, SLOTS // 32, hidden, 0)

    def product(role, half, m, cols=slice(None)):
        return jnp.dot(xt[m // 2, place_of(half, role)], acts[m, :, cols], preferred_element_type=F32)

    def put(role, u, v):
        v = v.astype(BF16)
        for i in range(v.shape[1] // BW):
            aa[role, 0, u + i] = v[:TOK, i * BW : (i + 1) * BW]
            aa[role, 1, u + i] = v[TOK:, i * BW : (i + 1) * BW]

    def send_far(u):
        send(aa.at[0, 0, u], rp.at[0, u], a2_send.at[0], far_sem.at[u], xm)
        send(aa.at[0, 1, u], rm.at[0, u], a2_send.at[1], far_sem.at[u], xp)

    def direct_up(u):
        send(aa.at[1, 0, u], rm.at[1, u], d_send.at[0], in_sem.at[u], xp)

    def direct_down(u):
        send(aa.at[2, 1, u], rp.at[1, u], d_send.at[1], in_sem.at[u], xm)

    def direct(u, carry):
        direct_up(u)
        direct_down(u)
        return carry

    def combine(u, carry):
        wait(aa.at[pl.ds(0, 2), 0, u], far_sem.at[u])
        aa[1, 1, u] = (aa[1, 1, u].astype(F32) + rm[0, u].astype(F32)).astype(BF16)
        send(aa.at[1, 1, u], rm.at[2, u], c_send.at[0], in_sem.at[u], xp)
        aa[2, 0, u] = (aa[2, 0, u].astype(F32) + rp[0, u].astype(F32)).astype(BF16)
        send(aa.at[2, 0, u], rp.at[2, u], c_send.at[1], in_sem.at[u], xm)
        return carry

    wait(gbuf.at[pl.ds(0, NEAR)], grecv.at[0])
    wait(gbuf.at[rest], grecv.at[1])

    def turn_dy(p, r0):
        rows = pl.ds(r0, 256)
        g = gbuf[rows, :].astype(F32)
        g = jnp.concatenate([g, g], axis=1)
        xt[1, block_of(p), :, rows] = (g * rbuf[NCH + p, rows, :].astype(F32)).astype(BF16).T

    def down_rows(p):
        return pl.ds(pl.multiple_of(block_of(p) * CW, CW), CW)

    def dy_near(p):
        k = NCH + p
        rows = pl.ds(0, NEAR)
        wait(rbuf.at[k, rows], rx.at[k])
        add_to(2, rows, p == 0, jnp.dot(rbuf[k, rows, :], wbuf[2, down_rows(p), :], preferred_element_type=F32))
        turn_dy(p, 0)

    def dy_far(p):
        k = NCH + p
        wait(rbuf.at[k, rest], rx2.at[k])
        add_to(2, rest, p == 0, jnp.dot(rbuf[k, rest, :], wbuf[2, down_rows(p), :], preferred_element_type=F32))
        turn_dy(p, 256)

    def dy_gradient(p):
        half, role = part_of(p)
        put(role, half * 3, product(role, half, 2))
        for i in range(3):
            u = half * 3 + i

            @pl.when(role == 0)
            def _():
                send_far(u)

            @pl.when(role == 1)
            def _():
                direct_up(u)

            @pl.when(role == 2)
            def _():
                direct_down(u)

        @pl.when(p == 2)
        def _():
            for i in range(3):
                combine(i, 0)

    def cotangents(j, carry):
        @pl.when(j + AHEAD < NCH)
        def _():
            own_out(NCH + AHEAD + j)

        @pl.when(j + 2 < NCH)
        def _():
            first(NCH + 2 + j)

        second(NCH + j)

        @pl.when(j >= 1)
        def _():
            dy_near(j - 1)

        @pl.when(j >= 2)
        def _():
            dy_far(j - 2)
            dy_gradient(j - 2)

        return carry

    lax.fori_loop(0, NCH, cotangents, 0)

    def pointwise(i, carry):
        rows = pl.ds(pl.multiple_of(i * 32, 32), 32)
        g = gbuf[rows, pl.ds(0, 1)].astype(F32)
        bg = acc[2, rows, :]
        gate = jnp.sum(bg * acts[2, rows, :].astype(F32), axis=1, keepdims=True)
        dh = g * bg
        acts[0, rows, :] = (dh * acc[0, rows, :]).astype(BF16)
        acts[1, rows, :] = (dh * acc[1, rows, :]).astype(BF16)
        rg[rows, pl.ds(D, TOK)] = jnp.broadcast_to(gate, (32, TOK)).astype(BF16)
        return carry

    def back(rows, n):
        nrow = pl.ds(pl.multiple_of(n * 256, 256), 256)
        dims = (((1,), (1,)), ((), ()))
        v = jnp.zeros((rows.size, 256), F32)
        for m in range(2):
            v = v + lax.dot_general(acts[m, rows, :], wbuf[m, nrow, :], dims, preferred_element_type=F32)
        rg[rows, nrow] = v.astype(BF16)

    def back_near(n, carry):
        back(pl.ds(0, NEAR), n)
        return carry

    def back_far(n, carry):
        back(rest, n)
        return carry

    def give_back(lo, hi, dy):
        for i in range(lo, hi):
            rows = pl.ds(i * CAP, CAP)
            if BLOCKS[i] == (0, 0, 0) and dy == 0:
                local(rg.at[rows], ret.at[rows], ret_sem)
            elif BLOCKS[i][0] == dy:
                send(rg.at[rows], ret.at[rows], ret_send, ret_sem, near(*BLOCKS[i]))

    dy_near(NCH - 1)
    lax.fori_loop(0, NEAR // 32, pointwise, 0)
    dy_far(NCH - 2)
    dy_far(NCH - 1)
    lax.fori_loop(NEAR // 32, SLOTS // 32, pointwise, 0)

    def gate_up(role, half):
        u = U0 + half * NA
        put(role, u, product(role, half, 0))
        put(role, u + 3, product(role, half, 1))

    def far_units(half, carry):
        gate_up(0, half)
        for i in range(NA):
            send_far(U0 + half * NA + i)
        return carry

    def beside(half, carry):
        for role in (1, 2):
            gate_up(role, half)
        return carry

    def own(half, carry):
        gate_up(3, half)
        return carry

    def total(u, h):
        s = aa[3, h, u].astype(F32) + rp[2 - h, u].astype(F32)
        return s + rm[1 + h, u].astype(F32)

    def arrived(u):
        wait(aa.at[:, 0, u], in_sem.at[u])

    def across(v, u):
        arrived(u)
        for h in range(2):
            ysend[v, h] = total(u, h).astype(BF16)
        send(ysend.at[v], yrecv.at[v], y_send, y_sem.at[v], yo)

    def across_down(i, carry):
        across(i, i)
        return carry


    def across_rest(i, carry):
        across(3 + i, U0 + i)
        return carry

    lax.fori_loop(0, 1, far_units, 0)
    dy_gradient(NCH - 2)
    lax.fori_loop(0, 3, across_down, 0)
    lax.fori_loop(0, D // 256, back_near, 0)
    give_back(0, NEAR // CAP, 1)
    lax.fori_loop(0, D // 256, back_far, 0)
    give_back(NEAR // CAP, SLOTS // CAP, 1)
    give_back(NEAR // CAP, SLOTS // CAP, 0)
    give_back(0, NEAR // CAP, 0)
    lax.fori_loop(3, 6, combine, 0)
    lax.fori_loop(0, 1, beside, 0)
    dy_gradient(NCH - 1)
    lax.fori_loop(U0, U0 + NA, direct, 0)
    lax.fori_loop(U0, U0 + NA, combine, 0)
    lax.fori_loop(1, 2, far_units, 0)
    lax.fori_loop(1, 2, beside, 0)
    lax.fori_loop(U0 + NA, NU, direct, 0)
    lax.fori_loop(0, 2, own, 0)
    lax.fori_loop(0, NA, across_rest, 0)
    lax.fori_loop(U0 + NA, NU, combine, 0)

    lane = lax.broadcasted_iota(jnp.int32, (1, SLOTS), 1)
    blk = lane // CAP
    expert = jnp.zeros((1, SLOTS), F32)
    for i, (dy, dz, dc) in enumerate(BLOCKS):
        expert = jnp.where(blk == i, exp_of(dy, -dz, dc).astype(F32), expert)
    slot = (lane - blk * CAP).astype(F32)
    ids_col = jnp.concatenate([mine_meta[...]] * (TOK // 8), axis=0).T
    h0 = jnp.where(ids_col[:, 0:1] == expert, 1.0, 0.0)
    h1 = jnp.where(ids_col[:, 1:2] == expert, 1.0, 0.0)
    after = jnp.where(row_i > col_i, 1.0, 0.0).astype(BF16)
    pos = jnp.dot(after, (h0 + h1).astype(BF16), preferred_element_type=F32)
    h0 = jnp.where(pos == slot, h0, 0.0).astype(BF16)
    h1 = jnp.where(pos == slot, h1, 0.0).astype(BF16)
    both = h0 + h1
    wait(ret, ret_sem)

    def gather(n, carry):
        ncol = pl.ds(pl.multiple_of(n * 256, 256), 256)
        ig_out[:, ncol] = jnp.dot(both, ret[:, ncol], preferred_element_type=F32).astype(BF16)
        return carry

    lax.fori_loop(0, D // 256, gather, 0)
    local(ig_out, ig_hbm, out_sem.at[0])
    g = ret[:, pl.ds(D, TOK)]
    g0 = jnp.dot(h0, g, preferred_element_type=F32).T
    g1 = jnp.dot(h1, g, preferred_element_type=F32).T
    gg_out[...] = jnp.concatenate([g0[0:1], g1[0:1]], axis=0).astype(BF16)
    local(gg_out, gg_hbm, out_sem.at[1])

    def finish(n, v, u):
        arrived(u)
        wait(yrecv.at[v], y_sem.at[v])
        for h in range(2):
            s = total(u, h) + yrecv[v, h].astype(F32)
            dl_out[n, pl.ds(h * TOK, TOK), :] = (s * 0.125).astype(BF16)
        local(dl_out.at[n], dl_hbm.at[n], out_sem.at[2])

    def finish_down(i, carry):
        finish(6 + i, i, 3 + i)
        return carry

    def finish_rest(i, carry):
        finish(i, 3 + i, U0 + NA + i)
        return carry

    lax.fori_loop(0, 3, finish_down, 0)
    lax.fori_loop(0, NA, finish_rest, 0)

    for i in range(4):
        wait(mine_meta, m_send.at[i])
    wait(stg1.at[pl.ds(1, 3)], st_send.at[0])
    wait(stg2.at[pl.ds(1, 3)], st_send.at[1])
    wait(stg3, st_send.at[2])
    wait(stg4, st_send.at[3])
    wait(gs1.at[pl.ds(1, 3)], gsend.at[0])
    wait(gs2.at[pl.ds(1, 3)], gsend.at[1])
    wait(gs3, gsend.at[2])
    wait(gs4, gsend.at[3])
    for i in range(2):
        wait(src.at[0], ring_send.at[i])
        wait(src.at[1], ring_send.at[2 + i])
        wait(aa.at[0, i], a2_send.at[i])
        wait(aa.at[0, i], d_send.at[i])
        wait(aa.at[0, i], c_send.at[i])
    wait(ysend, y_send)
    wait(rg.at[pl.ds(CAP, SLOTS - CAP)], ret_send)
    wait(ig_out, out_sem.at[0])
    wait(gg_out, out_sem.at[1])
    wait(dl_out, out_sem.at[2])


def place(ig, gg, dl, ig_out, gg_out, dg_out, du_out, dd_out, ig_v, gg_v, dl_v, in_sem, out_sem):
    def copies(out):
        pairs = [(ig, ig_v, ig_out), (gg, gg_v, gg_out)]
        for n in range(9):
            to = (dg_out, du_out, dd_out)[n // 3].at[0, :, pl.ds((n % 3) * BW, BW)]
            pairs.append((dl.at[n], dl_v.at[n], to))
        if out:
            return [pltpu.make_async_copy(v, o, out_sem.at[i]) for i, (_, v, o) in enumerate(pairs)]
        return [pltpu.make_async_copy(a, v, in_sem.at[i]) for i, (a, v, _) in enumerate(pairs)]

    ins, outs = copies(False), copies(True)
    for c in ins:
        c.start()
    for a, b in zip(ins, outs):
        a.wait()
        b.start()
    for c in outs:
        c.wait()


def on_device(features, out_grad, expert_ids, gate_probs, w_gate, w_up, w_down):
    vm, anyspace = pl.BlockSpec(memory_space=pltpu.VMEM), pl.BlockSpec(memory_space=pl.ANY)
    dma = pltpu.SemaphoreType.DMA
    ig, gg, dl = pl.pallas_call(
        kernel,
        name="moe",
        out_shape=(
            jax.ShapeDtypeStruct((TOK, D), BF16),
            jax.ShapeDtypeStruct((2, TOK), BF16),
            jax.ShapeDtypeStruct((9, 256, BW), BF16),
        ),
        in_specs=[anyspace, anyspace, vm, vm, anyspace, anyspace, anyspace],
        out_specs=(anyspace, anyspace, anyspace),
        scratch_shapes=[
            pltpu.VMEM((TOK, D), BF16),
            pltpu.VMEM((2, TOK), BF16),
            pltpu.VMEM((9, 256, BW), BF16),
            dma((3,)),
            pltpu.VMEM((5, 2 * NCH, TOK, CW), BF16),
            pltpu.VMEM((8, TOK), F32),
            pltpu.VMEM((4, 8, TOK), F32),
            pltpu.VMEM((3, 64, TOK), BF16),
            pltpu.VMEM((2, 160, TOK), BF16),
            pltpu.VMEM((4, 2 * NCH, 48, CW), BF16),
            pltpu.VMEM((4, 2 * NCH, 32, CW), BF16),
            pltpu.VMEM((2, 4, 2 * NCH, CAP, CW), BF16),
            pltpu.VMEM((2, 2, 2 * NCH, CAP, CW), BF16),
            pltpu.VMEM((4, 48, TOK), BF16),
            pltpu.VMEM((4, 32, TOK), BF16),
            pltpu.VMEM((2, 4, CAP, TOK), BF16),
            pltpu.VMEM((2, 2, CAP, TOK), BF16),
            pltpu.VMEM((2 * NCH, SLOTS, CW), BF16),
            pltpu.VMEM((SLOTS, TOK), BF16),
            pltpu.VMEM((3, D, FF), BF16),
            pltpu.VMEM((3, SLOTS, FF), F32),
            pltpu.VMEM((3, SLOTS, FF), BF16),
            pltpu.VMEM((2, NCH, CW, SLOTS), BF16),
            pltpu.VMEM((SLOTS, D + TOK), BF16),
            pltpu.VMEM((SLOTS, D + TOK), BF16),
            pltpu.VMEM((4, 2, NU, TOK, BW), BF16),
            pltpu.VMEM((3, NU, TOK, BW), BF16),
            pltpu.VMEM((3, NU, TOK, BW), BF16),
            pltpu.VMEM((3 + NA, 2, TOK, BW), BF16),
            pltpu.VMEM((3 + NA, 2, TOK, BW), BF16),
            dma((3,)),
            dma((3,)),
            dma((4,)),
            dma((4,)),
            dma((4,)),
            dma((2 * NCH,)),
            dma((2 * NCH,)),
            dma((4,)),
            dma((2 * NCH,)),
            dma((2 * NCH,)),
            dma((4,)),
            dma((2,)),
            dma((2,)),
            dma((2,)),
            dma((2,)),
            dma((NU,)),
            dma((NU,)),
            dma,
            dma((3 + NA,)),
            dma,
            dma,
            pltpu.SemaphoreType.REGULAR((4,)),
        ],
        compiler_params=pltpu.CompilerParams(
            collective_id=0, has_side_effects=True, vmem_limit_bytes=67_000_000
        ),
    )(features, out_grad, expert_ids.T, gate_probs.T, w_gate, w_up, w_down)
    delta = jax.ShapeDtypeStruct((1, 256, FF), BF16)
    ig, gg, d_gate, d_up, d_down = pl.pallas_call(
        place,
        name="place",
        out_shape=(
            jax.ShapeDtypeStruct((TOK, D), BF16),
            jax.ShapeDtypeStruct((2, TOK), BF16),
            delta,
            delta,
            delta,
        ),
        in_specs=[anyspace] * 3,
        out_specs=(anyspace,) * 5,
        scratch_shapes=[
            pltpu.VMEM((TOK, D), BF16),
            pltpu.VMEM((2, TOK), BF16),
            pltpu.VMEM((9, 256, BW), BF16),
            dma((11,)),
            dma((11,)),
        ],
    )(ig, gg, dl)
    return (ig, gg.T, d_gate, d_up, d_down)


def solution(mesh):
    rows = P(("rep", "exp"), None)
    weights = P("exp", None, None)
    deltas = P("exp", "rep", None)
    return jax.shard_map(
        on_device,
        mesh=mesh,
        in_specs=(rows, rows, rows, rows, weights, weights, weights),
        out_specs=(rows, rows, deltas, deltas, deltas),
        check_vma=False,
    )
```

```python
import functools

import jax
import jax.numpy as jnp
from jax import lax
from jax.experimental import pallas as pl
from jax.experimental.pallas import tpu as pltpu
from jax.sharding import PartitionSpec as P

MESH = pl.DeviceIdType.MESH
F32 = jnp.float32
BF16 = jnp.bfloat16
TOK = 128
D = 2048
FF = 768
CAP = 16
AHEAD = 4
NCH = 8
CW = D // NCH
SLOTS = 512
NEAR = 320
BW = 256
NA = 6
U0 = 6
NU = U0 + 2 * NA
QS = ((0, 0), (0, 1), (1, 0), (1, 1))
BLOCKS = tuple(
    [(dy, dz, dc) for dy, dc in QS for dz in (0, -1, 1, -2, 2)]
    + [(dy, -3, dc) for dy, dc in QS]
    + [(dy, 3, dc) for dy, dc in QS]
    + [(0, 4, dc) for dc in (0, 1)]
    + [(1, 4, dc) for dc in (0, 1)]
)


def kernel(
    feat, og, ids_row, gates_row, wg, wu, wd,
    ig_hbm, gg_hbm, dl_hbm,
    ig_out, gg_out, dl_out, out_sem,
    src, mine_meta, msrc, s1, s2, stg1, stg2, stg3, stg4, gs1, gs2, gs3, gs4, rbuf, gbuf,
    wbuf, acc, acts, xt, rg, ret, aa, rp, rm, ysend, yrecv,
    load_sem, w_sem, m_send, m_recv, ring_send, r1, r2, st_send, rx, rx2, gsend, grecv,
    a2_send, d_send, c_send, far_sem, in_sem, y_send, y_sem, ret_send, ret_sem, hop_sem,
):
    rep = lax.axis_index("rep")
    exp = lax.axis_index("exp")
    x = lax.rem(rep, 4)
    yh = rep // 4
    yl = exp // 16
    z = lax.rem(exp // 2, 8)
    c = lax.rem(exp, 2)

    def exp_of(dy, dz, dc):
        return lax.rem(yl + dy, 2) * 16 + lax.rem(z + dz + 8, 8) * 2 + lax.rem(c + dc, 2)

    def near(dy, dz, dc):
        return {"rep": rep, "exp": exp_of(dy, dz, dc)}

    xp = {"rep": yh * 4 + lax.rem(x + 1, 4), "exp": exp}
    xm = {"rep": yh * 4 + lax.rem(x + 3, 4), "exp": exp}
    yo = {"rep": (1 - yh) * 4 + x, "exp": exp}

    def send(a, b, ss, rs, to):
        pltpu.make_async_remote_copy(
            src_ref=a, dst_ref=b, send_sem=ss, recv_sem=rs, device_id=to, device_id_type=MESH
        ).start()

    def local(a, b, sem):
        pltpu.make_async_copy(a, b, sem).start()

    def wait(ref, sem):
        pltpu.make_async_copy(ref, ref, sem).wait()

    def place_of(half, role):
        return lax.rem(yh + 1 + half, 2) * 4 + lax.rem(x + 2 + 3 * role + 3 * (role * (role - 1) // 2), 4)

    def part_of(p):
        own = p // 6
        return own * (p - 6) + (1 - own) * (p // 3), own * 3 + (1 - own) * lax.rem(p, 3)

    def block_of(p):
        return place_of(*part_of(p))

    for k in range(NCH):
        local(feat.at[:, pl.ds(k * CW, CW)], src.at[0, k], load_sem.at[min(k, 1)])
    for k in range(NCH):
        cols = pl.ds(pl.multiple_of(block_of(k) * CW, CW), CW)
        local(og.at[:, cols], src.at[0, NCH + k], load_sem.at[2])
    for m, w in enumerate((wg, wu, wd)):
        local(w.at[0], wbuf.at[m], w_sem.at[m])

    mine_meta[...] = jnp.zeros_like(mine_meta)
    mine_meta[0:2, :] = ids_row[...].astype(F32)
    mine_meta[2:4, :] = gates_row[...].astype(F32)

    up, down = near(0, 1, 0), near(0, -1, 0)
    barrier = pltpu.get_barrier_semaphore()
    peers = [up, down] + [near(dy, 0, dc) for dy, dc in QS[1:]] + [xp, xm, yo]
    for p in peers:
        pl.semaphore_signal(barrier, inc=1, device_id=p, device_id_type=MESH)
    pl.semaphore_wait(barrier, len(peers))

    send(mine_meta, msrc.at[0], m_send.at[0], m_recv.at[0], up)
    send(mine_meta, msrc.at[1], m_send.at[1], m_recv.at[1], down)
    def own_out(k):
        send(src.at[0, k], src.at[1, k], ring_send.at[0], r1.at[k], up)
        send(src.at[0, k], src.at[2, k], ring_send.at[1], r1.at[k], down)

    wait(src.at[0, 0], load_sem.at[0])
    own_out(0)
    wait(src.at[0, pl.ds(1, NCH - 1)], load_sem.at[1])
    for k in range(1, NCH):
        own_out(k)
    wait(src.at[0, pl.ds(NCH, NCH)], load_sem.at[2])

    def greet(i):
        for p in (up, down):
            pl.semaphore_signal(hop_sem.at[i], inc=1, device_id=p, device_id_type=MESH)

    def greeted(i):
        pl.semaphore_wait(hop_sem.at[i], 2)

    greet(0)
    row_i = lax.broadcasted_iota(jnp.int32, (TOK, TOK), 0)
    col_i = lax.broadcasted_iota(jnp.int32, (TOK, TOK), 1)
    before = jnp.where(row_i < col_i, 1.0, 0.0).astype(BF16)
    slot_i = lax.broadcasted_iota(jnp.int32, (CAP, TOK), 0).astype(F32)

    def pick(meta_v, experts):
        i0, i1, g0, g1 = [jnp.broadcast_to(meta_v[i : i + 1, :], (CAP, TOK)) for i in range(4)]
        rows, gates = [], []
        for e in experts:
            ef = e.astype(F32)
            m0, m1 = i0 == ef, i1 == ef
            hit = jnp.where(m0 | m1, 1.0, 0.0)
            pos = jnp.dot(hit.astype(BF16), before, preferred_element_type=F32)
            one = jnp.where(pos == slot_i, hit, 0.0)
            gate = jnp.sum(one * jnp.where(m0, g0, jnp.where(m1, g1, 0.0)), axis=1, keepdims=True)
            rows.append(one.astype(BF16))
            gates.append(jnp.broadcast_to(gate, (CAP, TOK)).astype(BF16))
        return rows, gates

    own_plane = [exp_of(dy, 0, dc) for dy, dc in QS]

    def plan_first(s, meta_v):
        rows, gates = pick(meta_v, own_plane)
        for q in range(4):
            s1[s, pl.ds(q * CAP, CAP), :] = rows[q]
            gs1[q, pl.ds(s * CAP, CAP), :] = gates[q]

    plan_first(0, mine_meta[...])
    wait(msrc.at[0], m_recv.at[0])
    send(msrc.at[0], msrc.at[2], m_send.at[2], m_recv.at[2], up)
    wait(msrc.at[1], m_recv.at[1])
    send(msrc.at[1], msrc.at[3], m_send.at[3], m_recv.at[3], down)
    plan_first(1, msrc[0])
    plan_first(2, msrc[1])
    local(gs1.at[0], gbuf.at[pl.ds(0, 48)], grecv.at[0])
    for q in range(1, 4):
        send(gs1.at[q], gbuf.at[pl.ds(q * 80, 48)], gsend.at[0], grecv.at[0], near(QS[q][0], 0, QS[q][1]))

    def first(k):
        wait(src.at[pl.ds(1, 2), k], r1.at[k])
        send(src.at[1, k], src.at[3, k], ring_send.at[2], r2.at[k], up)
        send(src.at[2, k], src.at[4, k], ring_send.at[3], r2.at[k], down)
        for s in range(3):
            got = jnp.dot(s1[s], src[s, k], preferred_element_type=F32).astype(BF16)
            for q in range(4):
                stg1[q, k, pl.ds(s * CAP, CAP), :] = got[q * CAP : (q + 1) * CAP]
        local(stg1.at[0, k], rbuf.at[k, pl.ds(0, 48)], rx.at[k])
        for q in range(1, 4):
            send(stg1.at[q, k], rbuf.at[k, pl.ds(q * 80, 48)], st_send.at[0], rx.at[k], near(QS[q][0], 0, QS[q][1]))

    def first_x(k, carry):
        first(k)
        return carry

    for i in range(4):
        lax.fori_loop(2 * i, 2 * i + 2, first_x, 0)
        greeted(i)
        if i < 3:
            greet(i + 1)

    for d in range(2):
        step = 1 if d == 0 else -1
        wait(msrc.at[2 + d], m_recv.at[2 + d])
        third = [exp_of(dy, step, dc) for dy, dc in QS]
        fourth = [exp_of(d, 2 * step, dc) for dc in (0, 1)]
        rows, gates = pick(msrc[2 + d], own_plane + third + fourth)
        for i in range(10):
            s2[d, pl.ds(i * CAP, CAP), :] = rows[i]
        for q in range(4):
            gs2[q, pl.ds(d * CAP, CAP), :] = gates[q]
            gs3[d, q] = gates[4 + q]
        for i in range(2):
            gs4[d, i] = gates[8 + i]
    local(gs2.at[0], gbuf.at[pl.ds(48, 32)], grecv.at[0])
    for q in range(1, 4):
        send(gs2.at[q], gbuf.at[pl.ds(q * 80 + 48, 32)], gsend.at[1], grecv.at[0], near(QS[q][0], 0, QS[q][1]))
    for d in range(2):
        step = 1 if d == 0 else -1
        for q in range(4):
            send(gs3.at[d, q], gbuf.at[pl.ds(320 + (d * 4 + q) * CAP, CAP)], gsend.at[2], grecv.at[1], near(QS[q][0], step, QS[q][1]))
        for i in range(2):
            send(gs4.at[d, i], gbuf.at[pl.ds(448 + (d * 2 + i) * CAP, CAP)], gsend.at[3], grecv.at[1], near(d, 2 * step, i))

    def second(k):
        wait(src.at[pl.ds(3, 2), k], r2.at[k])
        for d in range(2):
            step = 1 if d == 0 else -1
            got = jnp.dot(s2[d], src[3 + d, k], preferred_element_type=F32).astype(BF16)
            for q in range(4):
                stg3[d, q, k] = got[(4 + q) * CAP : (5 + q) * CAP]
                stg2[q, k, pl.ds(d * CAP, CAP), :] = got[q * CAP : (q + 1) * CAP]
            for i in range(2):
                stg4[d, i, k] = got[(8 + i) * CAP : (9 + i) * CAP]
        local(stg2.at[0, k], rbuf.at[k, pl.ds(48, 32)], rx.at[k])
        for q in range(1, 4):
            send(stg2.at[q, k], rbuf.at[k, pl.ds(q * 80 + 48, 32)], st_send.at[1], rx.at[k], near(QS[q][0], 0, QS[q][1]))
        for d in range(2):
            step = 1 if d == 0 else -1
            for i in range(2):
                send(stg4.at[d, i, k], rbuf.at[k, pl.ds(448 + (d * 2 + i) * CAP, CAP)], st_send.at[3], rx2.at[k], near(d, 2 * step, i))
            for q in range(4):
                send(stg3.at[d, q, k], rbuf.at[k, pl.ds(320 + (d * 4 + q) * CAP, CAP)], st_send.at[2], rx2.at[k], near(QS[q][0], step, QS[q][1]))

    def second_x(k, carry):
        second(k)
        return carry

    lax.fori_loop(0, NCH, second_x, 0)
    for k in range(AHEAD):
        own_out(NCH + k)

    for m in range(3):
        wait(wbuf.at[m], w_sem.at[m])
    for k in range(NCH):
        wait(rbuf.at[k, pl.ds(0, NEAR)], rx.at[k])

    def near_x(n, carry):
        ncol = pl.ds(pl.multiple_of(n * 256, 256), 256)
        for m in range(2):
            v = jnp.zeros((NEAR, 256), F32)
            for k in range(NCH):
                v = v + jnp.dot(
                    rbuf[k, pl.ds(0, NEAR), :], wbuf[m, pl.ds(k * CW, CW), ncol], preferred_element_type=F32
                )
            acc[m, pl.ds(0, NEAR), ncol] = v
        return carry

    lax.fori_loop(0, FF // 256, near_x, 0)

    def turn_x(k, carry):
        xt[0, k, :, pl.ds(0, 256)] = rbuf[k, pl.ds(0, 256), :].T
        return carry

    lax.fori_loop(0, NCH, turn_x, 0)

    def hidden(i, carry):
        rows = pl.ds(pl.multiple_of(i * 32, 32), 32)
        pg, pu = acc[0, rows, :], acc[1, rows, :]
        sig = jax.nn.sigmoid(pg)
        act = pg * sig
        acts[2, rows, :] = (act * pu).astype(BF16)
        acc[0, rows, :] = pu * sig * (1.0 + pg * (1.0 - sig))
        acc[1, rows, :] = act
        return carry

    lax.fori_loop(0, NEAR // 32, hidden, 0)

    rest = pl.ds(NEAR, SLOTS - NEAR)

    def add_to(m, rows, first_one, part):
        @pl.when(first_one)
        def _():
            acc[m, rows, :] = part

        @pl.when(jnp.logical_not(first_one))
        def _():
            acc[m, rows, :] = acc[m, rows, :] + part

    def far_x(k, carry):
        wait(rbuf.at[k, rest], rx2.at[k])
        krow = pl.ds(pl.multiple_of(k * CW, CW), CW)
        for m in range(2):
            add_to(m, rest, k == 0, jnp.dot(rbuf[k, rest, :], wbuf[m, krow, :], preferred_element_type=F32))
        xt[0, k, :, pl.ds(256, 256)] = rbuf[k, pl.ds(256, 256), :].T
        return carry

    lax.fori_loop(0, NCH // 2, far_x, 0)
    first(NCH)
    lax.fori_loop(NCH // 2, NCH, far_x, 0)
    first(NCH + 1)
    lax.fori_loop(NEAR // 32, SLOTS // 32, hidden, 0)

    def product(role, half, m, cols=slice(None)):
        return jnp.dot(xt[m // 2, place_of(half, role)], acts[m, :, cols], preferred_element_type=F32)

    def put(role, u, v):
        v = v.astype(BF16)
        for i in range(v.shape[1] // BW):
            aa[role, 0, u + i] = v[:TOK, i * BW : (i + 1) * BW]
            aa[role, 1, u + i] = v[TOK:, i * BW : (i + 1) * BW]

    def send_far(u):
        send(aa.at[0, 0, u], rp.at[0, u], a2_send.at[0], far_sem.at[u], xm)
        send(aa.at[0, 1, u], rm.at[0, u], a2_send.at[1], far_sem.at[u], xp)

    def direct_up(u):
        send(aa.at[1, 0, u], rm.at[1, u], d_send.at[0], in_sem.at[u], xp)

    def direct_down(u):
        send(aa.at[2, 1, u], rp.at[1, u], d_send.at[1], in_sem.at[u], xm)

    def direct(u, carry):
        direct_up(u)
        direct_down(u)
        return carry

    def combine(u, carry):
        wait(aa.at[pl.ds(0, 2), 0, u], far_sem.at[u])
        aa[1, 1, u] = (aa[1, 1, u].astype(F32) + rm[0, u].astype(F32)).astype(BF16)
        send(aa.at[1, 1, u], rm.at[2, u], c_send.at[0], in_sem.at[u], xp)
        aa[2, 0, u] = (aa[2, 0, u].astype(F32) + rp[0, u].astype(F32)).astype(BF16)
        send(aa.at[2, 0, u], rp.at[2, u], c_send.at[1], in_sem.at[u], xm)
        return carry

    wait(gbuf.at[pl.ds(0, NEAR)], grecv.at[0])
    wait(gbuf.at[rest], grecv.at[1])

    def turn_dy(p, r0):
        rows = pl.ds(r0, 256)
        g = gbuf[rows, :].astype(F32)
        g = jnp.concatenate([g, g], axis=1)
        xt[1, block_of(p), :, rows] = (g * rbuf[NCH + p, rows, :].astype(F32)).astype(BF16).T

    def down_rows(p):
        return pl.ds(pl.multiple_of(block_of(p) * CW, CW), CW)

    def dy_near(p):
        k = NCH + p
        rows = pl.ds(0, NEAR)
        wait(rbuf.at[k, rows], rx.at[k])
        add_to(2, rows, p == 0, jnp.dot(rbuf[k, rows, :], wbuf[2, down_rows(p), :], preferred_element_type=F32))
        turn_dy(p, 0)

    def dy_far(p):
        k = NCH + p
        wait(rbuf.at[k, rest], rx2.at[k])
        add_to(2, rest, p == 0, jnp.dot(rbuf[k, rest, :], wbuf[2, down_rows(p), :], preferred_element_type=F32))
        turn_dy(p, 256)

    def dy_gradient(p):
        half, role = part_of(p)
        put(role, half * 3, product(role, half, 2))
        for i in range(3):
            u = half * 3 + i

            @pl.when(role == 0)
            def _():
                send_far(u)

            @pl.when(role == 1)
            def _():
                direct_up(u)

            @pl.when(role == 2)
            def _():
                direct_down(u)

        @pl.when(p == 2)
        def _():
            for i in range(3):
                combine(i, 0)

    def cotangents(j, carry):
        @pl.when(j + AHEAD < NCH)
        def _():
            own_out(NCH + AHEAD + j)

        @pl.when(j + 2 < NCH)
        def _():
            first(NCH + 2 + j)

        second(NCH + j)

        @pl.when(j >= 1)
        def _():
            dy_near(j - 1)

        @pl.when(j >= 2)
        def _():
            dy_far(j - 2)
            dy_gradient(j - 2)

        return carry

    lax.fori_loop(0, NCH, cotangents, 0)

    def pointwise(i, carry):
        rows = pl.ds(pl.multiple_of(i * 32, 32), 32)
        g = gbuf[rows, pl.ds(0, 1)].astype(F32)
        bg = acc[2, rows, :]
        gate = jnp.sum(bg * acts[2, rows, :].astype(F32), axis=1, keepdims=True)
        dh = g * bg
        acts[0, rows, :] = (dh * acc[0, rows, :]).astype(BF16)
        acts[1, rows, :] = (dh * acc[1, rows, :]).astype(BF16)
        rg[rows, pl.ds(D, TOK)] = jnp.broadcast_to(gate, (32, TOK)).astype(BF16)
        return carry

    def back(rows, n):
        nrow = pl.ds(pl.multiple_of(n * 256, 256), 256)
        dims = (((1,), (1,)), ((), ()))
        v = jnp.zeros((rows.size, 256), F32)
        for m in range(2):
            v = v + lax.dot_general(acts[m, rows, :], wbuf[m, nrow, :], dims, preferred_element_type=F32)
        rg[rows, nrow] = v.astype(BF16)

    def back_near(n, carry):
        back(pl.ds(0, NEAR), n)
        return carry

    def back_far(n, carry):
        back(rest, n)
        return carry

    def give_back(lo, hi, dy):
        for i in range(lo, hi):
            rows = pl.ds(i * CAP, CAP)
            if BLOCKS[i] == (0, 0, 0) and dy == 0:
                local(rg.at[rows], ret.at[rows], ret_sem)
            elif BLOCKS[i][0] == dy:
                send(rg.at[rows], ret.at[rows], ret_send, ret_sem, near(*BLOCKS[i]))

    dy_near(NCH - 1)
    lax.fori_loop(0, NEAR // 32, pointwise, 0)
    dy_far(NCH - 2)
    dy_far(NCH - 1)
    lax.fori_loop(NEAR // 32, SLOTS // 32, pointwise, 0)

    def gate_up(role, half):
        u = U0 + half * NA
        put(role, u, product(role, half, 0))
        put(role, u + 3, product(role, half, 1))

    def far_units(half, carry):
        gate_up(0, half)
        for i in range(NA):
            send_far(U0 + half * NA + i)
        return carry

    def beside(half, carry):
        for role in (1, 2):
            gate_up(role, half)
        return carry

    def own(half, carry):
        gate_up(3, half)
        return carry

    def total(u, h):
        s = aa[3, h, u].astype(F32) + rp[2 - h, u].astype(F32)
        return s + rm[1 + h, u].astype(F32)

    def arrived(u):
        wait(aa.at[:, 0, u], in_sem.at[u])

    def across(v, u):
        arrived(u)
        for h in range(2):
            ysend[v, h] = total(u, h).astype(BF16)
        send(ysend.at[v], yrecv.at[v], y_send, y_sem.at[v], yo)

    def across_down(i, carry):
        across(i, i)
        return carry


    def across_rest(i, carry):
        across(3 + i, U0 + i)
        return carry

    lax.fori_loop(0, 1, far_units, 0)
    dy_gradient(NCH - 2)
    lax.fori_loop(0, 3, across_down, 0)
    lax.fori_loop(0, D // 256, back_near, 0)
    give_back(0, NEAR // CAP, 1)
    lax.fori_loop(0, D // 256, back_far, 0)
    give_back(NEAR // CAP, SLOTS // CAP, 1)
    give_back(NEAR // CAP, SLOTS // CAP, 0)
    give_back(0, NEAR // CAP, 0)
    lax.fori_loop(3, 6, combine, 0)
    lax.fori_loop(0, 1, beside, 0)
    dy_gradient(NCH - 1)
    lax.fori_loop(U0, U0 + NA, direct, 0)
    lax.fori_loop(U0, U0 + NA, combine, 0)
    lax.fori_loop(1, 2, far_units, 0)
    lax.fori_loop(1, 2, beside, 0)
    lax.fori_loop(U0 + NA, NU, direct, 0)
    lax.fori_loop(0, 2, own, 0)
    lax.fori_loop(0, NA, across_rest, 0)
    lax.fori_loop(U0 + NA, NU, combine, 0)

    lane = lax.broadcasted_iota(jnp.int32, (1, SLOTS), 1)
    blk = lane // CAP
    expert = jnp.zeros((1, SLOTS), F32)
    for i, (dy, dz, dc) in enumerate(BLOCKS):
        expert = jnp.where(blk == i, exp_of(dy, -dz, dc).astype(F32), expert)
    slot = (lane - blk * CAP).astype(F32)
    ids_col = jnp.concatenate([mine_meta[...]] * (TOK // 8), axis=0).T
    h0 = jnp.where(ids_col[:, 0:1] == expert, 1.0, 0.0)
    h1 = jnp.where(ids_col[:, 1:2] == expert, 1.0, 0.0)
    after = jnp.where(row_i > col_i, 1.0, 0.0).astype(BF16)
    pos = jnp.dot(after, (h0 + h1).astype(BF16), preferred_element_type=F32)
    h0 = jnp.where(pos == slot, h0, 0.0).astype(BF16)
    h1 = jnp.where(pos == slot, h1, 0.0).astype(BF16)
    both = h0 + h1
    wait(ret, ret_sem)

    def gather(n, carry):
        ncol = pl.ds(pl.multiple_of(n * 256, 256), 256)
        ig_out[:, ncol] = jnp.dot(both, ret[:, ncol], preferred_element_type=F32).astype(BF16)
        return carry

    lax.fori_loop(0, D // 256, gather, 0)
    local(ig_out, ig_hbm, out_sem.at[0])
    g = ret[:, pl.ds(D, TOK)]
    g0 = jnp.dot(h0, g, preferred_element_type=F32).T
    g1 = jnp.dot(h1, g, preferred_element_type=F32).T
    gg_out[...] = jnp.concatenate([g0[0:1], g1[0:1]], axis=0).astype(BF16)
    local(gg_out, gg_hbm, out_sem.at[1])

    def finish(n, v, u):
        arrived(u)
        wait(yrecv.at[v], y_sem.at[v])
        for h in range(2):
            s = total(u, h) + yrecv[v, h].astype(F32)
            dl_out[n, pl.ds(h * TOK, TOK), :] = (s * 0.125).astype(BF16)
        local(dl_out.at[n], dl_hbm.at[n], out_sem.at[2])

    def finish_down(i, carry):
        finish(6 + i, i, 3 + i)
        return carry

    def finish_rest(i, carry):
        finish(i, 3 + i, U0 + NA + i)
        return carry

    lax.fori_loop(0, 3, finish_down, 0)
    lax.fori_loop(0, NA, finish_rest, 0)

    for i in range(4):
        wait(mine_meta, m_send.at[i])
    wait(stg1.at[pl.ds(1, 3)], st_send.at[0])
    wait(stg2.at[pl.ds(1, 3)], st_send.at[1])
    wait(stg3, st_send.at[2])
    wait(stg4, st_send.at[3])
    wait(gs1.at[pl.ds(1, 3)], gsend.at[0])
    wait(gs2.at[pl.ds(1, 3)], gsend.at[1])
    wait(gs3, gsend.at[2])
    wait(gs4, gsend.at[3])
    for i in range(2):
        wait(src.at[0], ring_send.at[i])
        wait(src.at[1], ring_send.at[2 + i])
        wait(aa.at[0, i], a2_send.at[i])
        wait(aa.at[0, i], d_send.at[i])
        wait(aa.at[0, i], c_send.at[i])
    wait(ysend, y_send)
    wait(rg.at[pl.ds(CAP, SLOTS - CAP)], ret_send)
    wait(ig_out, out_sem.at[0])
    wait(gg_out, out_sem.at[1])
    wait(dl_out, out_sem.at[2])


def place(ig, gg, dl, ig_out, gg_out, dg_out, du_out, dd_out, ig_v, gg_v, dl_v, in_sem, out_sem):
    def copies(out):
        pairs = [(ig, ig_v, ig_out), (gg, gg_v, gg_out)]
        for n in range(9):
            to = (dg_out, du_out, dd_out)[n // 3].at[0, :, pl.ds((n % 3) * BW, BW)]
            pairs.append((dl.at[n], dl_v.at[n], to))
        if out:
            return [pltpu.make_async_copy(v, o, out_sem.at[i]) for i, (_, v, o) in enumerate(pairs)]
        return [pltpu.make_async_copy(a, v, in_sem.at[i]) for i, (a, v, _) in enumerate(pairs)]

    ins, outs = copies(False), copies(True)
    for c in ins:
        c.start()
    for a, b in zip(ins, outs):
        a.wait()
        b.start()
    for c in outs:
        c.wait()


def on_device(features, out_grad, expert_ids, gate_probs, w_gate, w_up, w_down):
    vm, anyspace = pl.BlockSpec(memory_space=pltpu.VMEM), pl.BlockSpec(memory_space=pl.ANY)
    dma = pltpu.SemaphoreType.DMA
    ig, gg, dl = pl.pallas_call(
        kernel,
        name="moe",
        out_shape=(
            jax.ShapeDtypeStruct((TOK, D), BF16),
            jax.ShapeDtypeStruct((2, TOK), BF16),
            jax.ShapeDtypeStruct((9, 256, BW), BF16),
        ),
        in_specs=[anyspace, anyspace, vm, vm, anyspace, anyspace, anyspace],
        out_specs=(anyspace, anyspace, anyspace),
        scratch_shapes=[
            pltpu.VMEM((TOK, D), BF16),
            pltpu.VMEM((2, TOK), BF16),
            pltpu.VMEM((9, 256, BW), BF16),
            dma((3,)),
            pltpu.VMEM((5, 2 * NCH, TOK, CW), BF16),
            pltpu.VMEM((8, TOK), F32),
            pltpu.VMEM((4, 8, TOK), F32),
            pltpu.VMEM((3, 64, TOK), BF16),
            pltpu.VMEM((2, 160, TOK), BF16),
            pltpu.VMEM((4, 2 * NCH, 48, CW), BF16),
            pltpu.VMEM((4, 2 * NCH, 32, CW), BF16),
            pltpu.VMEM((2, 4, 2 * NCH, CAP, CW), BF16),
            pltpu.VMEM((2, 2, 2 * NCH, CAP, CW), BF16),
            pltpu.VMEM((4, 48, TOK), BF16),
            pltpu.VMEM((4, 32, TOK), BF16),
            pltpu.VMEM((2, 4, CAP, TOK), BF16),
            pltpu.VMEM((2, 2, CAP, TOK), BF16),
            pltpu.VMEM((2 * NCH, SLOTS, CW), BF16),
            pltpu.VMEM((SLOTS, TOK), BF16),
            pltpu.VMEM((3, D, FF), BF16),
            pltpu.VMEM((3, SLOTS, FF), F32),
            pltpu.VMEM((3, SLOTS, FF), BF16),
            pltpu.VMEM((2, NCH, CW, SLOTS), BF16),
            pltpu.VMEM((SLOTS, D + TOK), BF16),
            pltpu.VMEM((SLOTS, D + TOK), BF16),
            pltpu.VMEM((4, 2, NU, TOK, BW), BF16),
            pltpu.VMEM((3, NU, TOK, BW), BF16),
            pltpu.VMEM((3, NU, TOK, BW), BF16),
            pltpu.VMEM((3 + NA, 2, TOK, BW), BF16),
            pltpu.VMEM((3 + NA, 2, TOK, BW), BF16),
            dma((3,)),
            dma((3,)),
            dma((4,)),
            dma((4,)),
            dma((4,)),
            dma((2 * NCH,)),
            dma((2 * NCH,)),
            dma((4,)),
            dma((2 * NCH,)),
            dma((2 * NCH,)),
            dma((4,)),
            dma((2,)),
            dma((2,)),
            dma((2,)),
            dma((2,)),
            dma((NU,)),
            dma((NU,)),
            dma,
            dma((3 + NA,)),
            dma,
            dma,
            pltpu.SemaphoreType.REGULAR((4,)),
        ],
        compiler_params=pltpu.CompilerParams(
            collective_id=0, has_side_effects=True, vmem_limit_bytes=67_000_000
        ),
    )(features, out_grad, expert_ids.T, gate_probs.T, w_gate, w_up, w_down)
    delta = jax.ShapeDtypeStruct((1, 256, FF), BF16)
    ig, gg, d_gate, d_up, d_down = pl.pallas_call(
        place,
        name="place",
        out_shape=(
            jax.ShapeDtypeStruct((TOK, D), BF16),
            jax.ShapeDtypeStruct((2, TOK), BF16),
            delta,
            delta,
            delta,
        ),
        in_specs=[anyspace] * 3,
        out_specs=(anyspace,) * 5,
        scratch_shapes=[
            pltpu.VMEM((TOK, D), BF16),
            pltpu.VMEM((2, TOK), BF16),
            pltpu.VMEM((9, 256, BW), BF16),
            dma((11,)),
            dma((11,)),
        ],
    )(ig, gg, dl)
    return (ig, gg.T, d_gate, d_up, d_down)


def solution(mesh):
    rows = P(("rep", "exp"), None)
    weights = P("exp", None, None)
    deltas = P("exp", "rep", None)
    return jax.shard_map(
        on_device,
        mesh=mesh,
        in_specs=(rows, rows, rows, rows, weights, weights, weights),
        out_specs=(rows, rows, deltas, deltas, deltas),
        check_vma=False,
    )
```
